512 devices in a mesh: shard: 128 (over y, z, core), tensor: 4 (over x).
Axes of the slice: x: 4, y: 4, z: 16, core: 2. Of those that a mesh axis runs over, the one named last changes fastest.
Arguments:
- expert_grads: bfloat16 [2, 128, 2, 512, 1024], P(None, 'shard', None, None, 'tensor')
- embed_grads: bfloat16 [2, 128, 4096, 512], P(None, 'shard', None, 'tensor')
- small_grads: bfloat16 [2, 128, 512, 36], P(None, 'shard', None, 'tensor')
- expert_master: float32 [2, 512, 1024], P(None, 'shard', 'tensor'), may hold values from -0.2 to 0.2
- expert_first: float32 [2, 512, 1024], P(None, 'shard', 'tensor'), may hold values from -6 to 6
- expert_second: float32 [2, 512, 1024], P(None, 'shard', 'tensor'), may hold values from 0.02 to 0.2
- embed_master: float32 [4096, 512], P('shard', 'tensor'), may hold values from -0.2 to 0.2
- embed_first: float32 [4096, 512], P('shard', 'tensor'), may hold values from -6 to 6
- embed_second: float32 [4096, 512], P('shard', 'tensor'), may hold values from 0.02 to 0.2
- small_master: float32 [512, 36], P('shard', 'tensor'), may hold values from -0.2 to 0.2
- small_first: float32 [512, 36], P('shard', 'tensor'), may hold values from -6 to 6
- small_second: float32 [512, 36], P('shard', 'tensor'), may hold values from 0.02 to 0.2
- class_steps: int32 [4096], P('shard'), may hold values from 1 to 2000
- clip_rms: float32 [], replicated, may hold values from 1 to 1.5
Outputs:
- expert_weights: bfloat16 [2, 512, 1024], P(None, None, 'tensor')
- embed_weights: bfloat16 [4096, 512], P(None, 'tensor')
- small_weights: bfloat16 [512, 36], P(None, 'tensor')
- expert_master_new: float32 [2, 512, 1024], P(None, 'shard', 'tensor')
- expert_first_new: float32 [2, 512, 1024], P(None, 'shard', 'tensor')
- expert_second_new: float32 [2, 512, 1024], P(None, 'shard', 'tensor')
- embed_master_new: float32 [4096, 512], P('shard', 'tensor')
- embed_first_new: float32 [4096, 512], P('shard', 'tensor')
- embed_second_new: float32 [4096, 512], P('shard', 'tensor')
- embed_step: float32 [4096, 512], P('shard', 'tensor')
- small_master_new: float32 [512, 36], P('shard', 'tensor')
- small_first_new: float32 [512, 36], P('shard', 'tensor')
- small_second_new: float32 [512, 36], P('shard', 'tensor')
- clip_scale: float32 [], replicated
The draws below stay inside these ranges and needn't reach their ends.
All inputs are finite; a program needn't handle non-finite values.
Results may differ from the reference program's by a relative error of at most 0.001.
Values may be sent and summed in bfloat16 or wider, within the bound.
No kernel may reach another device: no remote copies, remote signals or barrier semaphores. Data moves between devices by JAX's collectives and lax.ppermute only.
A program may use at most 64 MiB of HBM per device.

```python
import math
import jax
import jax.numpy as jnp
from jax import lax

D = 512
FFW = 1024
CLASSES = 4096
SMALL = 36
MICRO = 2
STEP = 1000
SHARDS = 128
P_TOT = 3164160


def rough_gradient(key, shape, gain, sparse):
    rows = shape[-2]
    cols = shape[-1]
    noise_key = jax.random.fold_in(key, 0)
    row_key = jax.random.fold_in(key, 1)
    col_key = jax.random.fold_in(key, 2)
    keep_key = jax.random.fold_in(key, 4)
    rise = 3.0 ** (jnp.arange(rows, dtype=jnp.float32) / rows)
    row_rand = 10.0 ** (jax.random.uniform(row_key, (rows,), jnp.float32) - 0.5)
    col_rand = 3.0 ** (jax.random.uniform(col_key, (cols,), jnp.float32) - 0.5)
    scale = gain * (rise * row_rand)[:, None] * col_rand[None, :] / jnp.sqrt(2.0 * SHARDS)
    noise = jax.random.normal(noise_key, shape, jnp.float32)
    values = noise * scale
    if sparse:
        picks = jax.random.randint(keep_key, shape[:-1], 0, 8)
        keep = jnp.where(picks == 0, jnp.float32(2.8284271), jnp.float32(0.0))
        values = values * keep[..., None]
    return values


def master_values(key, shape):
    values = 0.05 * jax.random.normal(key, shape, jnp.float32)
    return jnp.clip(values, -0.2, 0.2)


def draw_expert_grads(key, part):
    return rough_gradient(jax.random.fold_in(key, 11), (MICRO, SHARDS, 2, D, FFW), 1.0, False).astype(jnp.bfloat16)


def draw_embed_grads(key, part):
    return rough_gradient(jax.random.fold_in(key, 12), (MICRO, SHARDS, CLASSES, D), 1.0, True).astype(jnp.bfloat16)


def draw_small_grads(key, part):
    return rough_gradient(jax.random.fold_in(key, 13), (MICRO, SHARDS, D, SMALL), 10.0, False).astype(jnp.bfloat16)


def draw_expert_master(key, part):
    return master_values(jax.random.fold_in(key, 21), (2, D, FFW))


def draw_embed_master(key, part):
    return master_values(jax.random.fold_in(key, 22), (CLASSES, D))


def draw_small_master(key, part):
    return master_values(jax.random.fold_in(key, 23), (D, SMALL))


def plant(result, own_key, least, top_value):
    index_at = [jax.random.randint(jax.random.fold_in(own_key, axis), (), 0, length) for axis, length in enumerate(result.shape)]
    main_axis = result.shape.index(max(result.shape))
    next_to = index_at[:main_axis] + [(index_at[main_axis] + 1) % result.shape[main_axis]] + index_at[main_axis + 1:]
    return result.at[tuple(index_at)].set(least).at[tuple(next_to)].set(top_value)


def shard_levels(stream_key, dims, cuts, least, top_value):
    def one(axis_at, shards_of):
        heights = jax.random.uniform(jax.random.fold_in(jax.random.fold_in(stream_key, 6), axis_at), (shards_of,), jnp.float32, least / len(cuts), top_value / len(cuts))
        return jnp.repeat(jnp.exp(heights), dims[axis_at] // shards_of).reshape((-1,) + (1,) * (len(dims) - axis_at - 1))

    factor_of = one(*cuts[0])
    for cut in cuts[1:]:
        factor_of = factor_of * one(*cut)
    return factor_of


def centred(key, shape, width, most, pieces=(), kind=jnp.bfloat16):
    drawn = jax.random.normal(key, shape, jnp.float32) * width
    if len(pieces) > 0:
        drawn = shard_levels(key, shape, pieces, -0.22, 0.18) * drawn
    return jnp.clip(drawn, min=-most, max=most).astype(kind)


def setup_inputs(seed: int = 0) -> dict:
    splits = jax.random.split(jax.random.key(seed), 15)
    return {
        "expert_grads": draw_expert_grads(jax.random.fold_in(splits[14], 71), 0),
        "embed_grads": draw_embed_grads(jax.random.fold_in(splits[14], 71), 0),
        "small_grads": draw_small_grads(jax.random.fold_in(splits[14], 71), 0),
        "expert_master": draw_expert_master(jax.random.fold_in(splits[14], 71), 0),
        "expert_first": centred(splits[4], (2, D, FFW), 1.0, 6.0, ((1, 128), (2, 4)), jnp.float32),
        "expert_second": jnp.clip(jnp.exp(math.log(0.2) - 2.3025851 * jax.random.uniform(splits[5], (2, D, FFW), jnp.float32) ** shard_levels(splits[5], (2, D, FFW), ((1, 128), (2, 4)), -0.2, 0.2)), 0.02, 0.2),
        "embed_master": draw_embed_master(jax.random.fold_in(splits[14], 71), 0),
        "embed_first": centred(splits[7], (CLASSES, D), 1.0, 6.0, ((0, 128), (1, 4)), jnp.float32),
        "embed_second": jnp.clip(jnp.exp(math.log(0.2) - 2.3025851 * jax.random.uniform(splits[8], (CLASSES, D), jnp.float32) ** shard_levels(splits[8], (CLASSES, D), ((0, 128), (1, 4)), -0.2, 0.2)), 0.02, 0.2),
        "small_master": draw_small_master(jax.random.fold_in(splits[14], 71), 0),
        "small_first": centred(splits[10], (D, SMALL), 1.0, 6.0, ((0, 128), (1, 4)), jnp.float32),
        "small_second": jnp.clip(jnp.exp(math.log(0.2) - 2.3025851 * jax.random.uniform(splits[11], (D, SMALL), jnp.float32) ** shard_levels(splits[11], (D, SMALL), ((0, 128), (1, 4)), -0.2, 0.2)), 0.02, 0.2),
        "class_steps": plant(jax.random.randint(splits[12], (CLASSES,), 1, 2001), jax.random.fold_in(splits[12], 1), 1, 2000).astype(jnp.int32),
        "clip_rms": jnp.clip(jax.random.uniform(splits[13], (), jnp.float32, 1.0, 1.5), 1.0, 1.5),
    }


BETA_ONE = 0.9
BETA_TWO = 0.999
LEARN_RATE = 0.001
DECAY_RATE = 0.1
EPSILON = 1e-08

def contributions(gradients):

    def add_one(summed, shard_index):
        piece = lax.dynamic_index_in_dim(gradients, shard_index, 1, keepdims=False)
        return (summed + lax.optimization_barrier(jnp.sum(piece.astype(jnp.float32), axis=0)), None)
    start = jnp.zeros(gradients.shape[2:], jnp.float32)
    summed, _ = lax.scan(add_one, start, jnp.arange(gradients.shape[1], dtype=jnp.int32))
    return summed

def adam_rule(summed, master, first_moment, second_moment, clip_factor, corr_one, corr_two):
    scaled = clip_factor * summed
    first_new = BETA_ONE * first_moment + (1.0 - BETA_ONE) * scaled
    second_new = BETA_TWO * second_moment + (1.0 - BETA_TWO) * scaled * scaled
    update_step = first_new / corr_one / (jnp.sqrt(second_new / corr_two) + EPSILON) + DECAY_RATE * master
    master_new = master - LEARN_RATE * update_step
    return (master_new, first_new, second_new, update_step)

def reference(expert_grads, embed_grads, small_grads, expert_master, expert_first, expert_second, embed_master, embed_first, embed_second, small_master, small_first, small_second, class_steps, clip_rms):
    expert_sum = contributions(expert_grads)
    embed_sum = contributions(embed_grads)
    small_sum = contributions(small_grads)
    squares = jnp.sum(expert_sum * expert_sum) + jnp.sum(embed_sum * embed_sum) + jnp.sum(small_sum * small_sum)
    clip_factor = clip_rms * jnp.sqrt(P_TOT / squares)
    fixed_one = 1.0 - BETA_ONE ** STEP
    fixed_two = 1.0 - BETA_TWO ** STEP
    row_float = class_steps.astype(jnp.float32)[:, None]
    row_one = 1.0 - BETA_ONE ** row_float
    row_two = 1.0 - BETA_TWO ** row_float
    expert_out = adam_rule(expert_sum, expert_master, expert_first, expert_second, clip_factor, fixed_one, fixed_two)
    embed_out = adam_rule(embed_sum, embed_master, embed_first, embed_second, clip_factor, row_one, row_two)
    small_out = adam_rule(small_sum, small_master, small_first, small_second, clip_factor, fixed_one, fixed_two)
    return (expert_out[0].astype(jnp.bfloat16), embed_out[0].astype(jnp.bfloat16), small_out[0].astype(jnp.bfloat16), expert_out[0], expert_out[1], expert_out[2], embed_out[0], embed_out[1], embed_out[2], embed_out[3], small_out[0], small_out[1], small_out[2], clip_factor)
```

```python
import jax
import jax.numpy as jnp
from jax import lax
from jax.sharding import Mesh, PartitionSpec as P

STEP = 1000
P_TOT = 3164160

BETA_ONE = 0.9
BETA_TWO = 0.999
LEARN_RATE = 0.001
DECAY_RATE = 0.1
EPSILON = 1e-08

Y, Z, C, T = 4, 16, 2, 4


def local_total(gradients):
    return gradients[0, 0].astype(jnp.float32) + gradients[1, 0].astype(jnp.float32)


def finish(first_new, second_new, master, corr_one, corr_two):
    update_step = (
        first_new / corr_one / (jnp.sqrt(second_new / corr_two) + EPSILON) + DECAY_RATE * master
    )
    master_new = master - LEARN_RATE * update_step
    return (master_new, update_step)


def pack_expert(x):
    return x.reshape(2, 4, 2, 128).transpose(0, 2, 1, 3).reshape(16, 128)


def unpack_expert(x):
    return x.reshape(2, 2, 4, 128).transpose(0, 2, 1, 3).reshape(2, 4, 256)


def exchange(x, axes):
    return lax.all_to_all(x, axes, 0, 0, tiled=True)


def spread(x, n, axes):
    return exchange(jnp.broadcast_to(x[None], (n,) + x.shape), axes)


def body(
    expert_grads,
    embed_grads,
    small_grads,
    expert_master,
    expert_first,
    expert_second,
    embed_master,
    embed_first,
    embed_second,
    small_master,
    small_first,
    small_second,
    class_steps,
    clip_rms,
):
    e = local_total(expert_grads).reshape(2, Y, Z, C, 4, 2, 128)
    e = e.transpose(3, 1, 2, 0, 5, 4, 6).reshape(C, Y, Z, 16, 128)
    m = local_total(embed_grads).reshape(Y, Z, C, 32, 128).transpose(2, 0, 1, 3, 4)
    s = local_total(small_grads).reshape(Y, Z, C, 4, 9).transpose(2, 0, 1, 3, 4)
    s = jnp.pad(s, ((0, 0),) * 3 + ((0, 4), (0, 119)))
    buf = jnp.concatenate([m, e, s], axis=3)
    got = exchange(buf, ("c",))
    part = got[0] + got[1]
    big = part[:, :, :48].astype(jnp.bfloat16)
    small_part = part[:, :, 48:52]
    high = lax.reduce_precision(small_part, 8, 7)
    low = (small_part - high).astype(jnp.bfloat16)
    got = exchange(jnp.concatenate([big, high.astype(jnp.bfloat16), low], axis=2), ("y",))
    got = got.astype(jnp.float32)
    part = got[0] + got[1] + got[2] + got[3]
    part = jnp.concatenate([part[:, :48], part[:, 48:52] + part[:, 52:56], jnp.zeros((Z, 4, 128), jnp.float32)], axis=1)
    got = exchange(part, ("z",))
    total = jnp.sum(got, axis=0)
    squares = jnp.sum(total * total)
    line = jnp.broadcast_to(squares, (Y * C * T, 128))
    line = exchange(line, ("y", "c", "t"))
    line = jnp.broadcast_to(jnp.sum(line, axis=0)[None], (Z, 128))
    total_squares = jnp.sum(exchange(line, ("z",))[:, 0])
    clip_factor = clip_rms * jnp.sqrt(P_TOT / total_squares)

    embed_sum = total[:32]
    expert_sum = unpack_expert(total[32:48])
    small_sum = total[48:52, :9]
    summed_all = (expert_sum, embed_sum, small_sum)

    def moments(group_index, first_moment, second_moment):
        scaled = clip_factor * summed_all[group_index]
        return (
            BETA_ONE * first_moment + (1.0 - BETA_ONE) * scaled,
            BETA_TWO * second_moment + (1.0 - BETA_TWO) * scaled * scaled,
        )

    fixed_one = 1.0 - BETA_ONE**STEP
    fixed_two = 1.0 - BETA_TWO**STEP
    row_float = class_steps.astype(jnp.float32)[:, None]
    row_one = 1.0 - BETA_ONE**row_float
    row_two = 1.0 - BETA_TWO**row_float
    expert_first_new, expert_second_new = moments(0, expert_first, expert_second)
    embed_first_new, embed_second_new = moments(1, embed_first, embed_second)
    small_first_new, small_second_new = moments(2, small_first, small_second)
    expert_master_new, expert_update = finish(
        expert_first_new, expert_second_new, expert_master, fixed_one, fixed_two
    )
    embed_master_new, embed_update = finish(
        embed_first_new, embed_second_new, embed_master, row_one, row_two
    )
    small_master_new, small_update = finish(
        small_first_new, small_second_new, small_master, fixed_one, fixed_two
    )
    own = jnp.concatenate(
        [
            embed_master_new.astype(jnp.bfloat16),
            pack_expert(expert_master_new.astype(jnp.bfloat16)),
            jnp.pad(small_master_new.astype(jnp.bfloat16), ((0, 4), (0, 119))),
        ],
        axis=0,
    )
    full = spread(own, Z, ("z",))
    full = spread(full, Y, ("y",))
    full = spread(full, C, ("c",))
    full = full.transpose(1, 2, 0, 3, 4)
    embed_weights = full[:, :, :, :32].reshape(4096, 128)
    expert_weights = full[:, :, :, 32:48].reshape(Y, Z, C, 2, 2, 4, 128)
    expert_weights = expert_weights.transpose(3, 0, 1, 2, 5, 4, 6).reshape(2, 512, 256)
    small_weights = full[:, :, :, 48:52, :9].reshape(512, 9)
    return (
        expert_weights,
        embed_weights,
        small_weights,
        expert_master_new,
        expert_first_new,
        expert_second_new,
        embed_master_new,
        embed_first_new,
        embed_second_new,
        embed_update,
        small_master_new,
        small_first_new,
        small_second_new,
        clip_factor,
    )


def solution(mesh):
    fine = Mesh(mesh.devices.reshape(Y, Z, C, T), ("y", "z", "c", "t"))
    sh = ("y", "z", "c")
    in_specs = (
        P(None, sh, None, None, "t"),
        P(None, sh, None, "t"),
        P(None, sh, None, "t"),
        P(None, sh, "t"),
        P(None, sh, "t"),
        P(None, sh, "t"),
        P(sh, "t"),
        P(sh, "t"),
        P(sh, "t"),
        P(sh, "t"),
        P(sh, "t"),
        P(sh, "t"),
        P(sh),
        P(),
    )
    out_specs = (
        P(None, None, "t"),
        P(None, "t"),
        P(None, "t"),
        P(None, sh, "t"),
        P(None, sh, "t"),
        P(None, sh, "t"),
        P(sh, "t"),
        P(sh, "t"),
        P(sh, "t"),
        P(sh, "t"),
        P(sh, "t"),
        P(sh, "t"),
        P(sh, "t"),
        P(),
    )
    return jax.shard_map(body, mesh=fine, in_specs=in_specs, out_specs=out_specs, check_vma=False)
```

```python
import jax
import jax.numpy as jnp
from jax import lax
from jax.sharding import Mesh, PartitionSpec as P

STEP = 1000
P_TOT = 3164160

BETA_ONE = 0.9
BETA_TWO = 0.999
LEARN_RATE = 0.001
DECAY_RATE = 0.1
EPSILON = 1e-08

Y, ZH, ZL, C, T = 4, 8, 2, 2, 4
Z = ZH * ZL
NEAR = ("y", "w")


def local_total(gradients):
    return gradients[0, 0].astype(jnp.float32) + gradients[1, 0].astype(jnp.float32)


def finish(first_new, second_new, master, corr_one, corr_two):
    update_step = (
        first_new / corr_one / (jnp.sqrt(second_new / corr_two) + EPSILON) + DECAY_RATE * master
    )
    master_new = master - LEARN_RATE * update_step
    return (master_new, update_step)


def pack_expert(x):
    return x.reshape(2, 4, 2, 128).transpose(0, 2, 1, 3).reshape(16, 128)


def unpack_expert(x):
    return x.reshape(2, 2, 4, 128).transpose(0, 2, 1, 3).reshape(2, 4, 256)


def exchange(x, axes):
    return lax.all_to_all(x, axes, 0, 0, tiled=True)


def spread(x, n, axes):
    return exchange(jnp.broadcast_to(x[None], (n,) + x.shape), axes)


def body(
    expert_grads,
    embed_grads,
    small_grads,
    expert_master,
    expert_first,
    expert_second,
    embed_master,
    embed_first,
    embed_second,
    small_master,
    small_first,
    small_second,
    class_steps,
    clip_rms,
):
    e = local_total(expert_grads).reshape(2, Y, ZH, ZL, C, 4, 2, 128)
    e = e.transpose(4, 1, 3, 2, 0, 6, 5, 7).reshape(C, Y * ZL, ZH, 16, 128)
    m = local_total(embed_grads).reshape(Y, ZH, ZL, C, 32, 128)
    m = m.transpose(3, 0, 2, 1, 4, 5).reshape(C, Y * ZL, ZH, 32, 128)
    s = local_total(small_grads).reshape(Y, ZH, ZL, C, 4, 9)
    s = s.transpose(3, 0, 2, 1, 4, 5).reshape(C, Y * ZL, ZH, 4, 9)
    s = jnp.pad(s, ((0, 0),) * 3 + ((0, 4), (0, 119)))
    buf = jnp.concatenate([m, e, s], axis=3)
    got = exchange(buf, ("c",))
    part = got[0] + got[1]
    big = part[:, :, :48].astype(jnp.bfloat16)
    small_part = part[:, :, 48:52]
    high = lax.reduce_precision(small_part, 8, 7)
    low = (small_part - high).astype(jnp.bfloat16)
    got = exchange(jnp.concatenate([big, high.astype(jnp.bfloat16), low], axis=2), NEAR)
    part = jnp.sum(got.astype(jnp.float32), axis=0)
    part = jnp.concatenate(
        [part[:, :48], part[:, 48:52] + part[:, 52:56], jnp.zeros((ZH, 4, 128), jnp.float32)],
        axis=1,
    )
    total = jnp.sum(exchange(part.reshape(ZH, 56, 128), ("z",)), axis=0)
    squares = jnp.sum(total * total)
    line = jnp.broadcast_to(squares, (Y * ZL * C * T, 128))
    line = exchange(line, NEAR + ("c", "t"))
    line = jnp.broadcast_to(jnp.sum(line, axis=0)[None], (ZH, 128))
    total_squares = jnp.sum(exchange(line, ("z",))[:, 0])
    clip_factor = clip_rms * jnp.sqrt(P_TOT / total_squares)

    embed_sum = total[:32]
    expert_sum = unpack_expert(total[32:48])
    small_sum = total[48:52, :9]
    summed_all = (expert_sum, embed_sum, small_sum)

    def moments(group_index, first_moment, second_moment):
        scaled = clip_factor * summed_all[group_index]
        return (
            BETA_ONE * first_moment + (1.0 - BETA_ONE) * scaled,
            BETA_TWO * second_moment + (1.0 - BETA_TWO) * scaled * scaled,
        )

    fixed_one = 1.0 - BETA_ONE**STEP
    fixed_two = 1.0 - BETA_TWO**STEP
    row_float = class_steps.astype(jnp.float32)[:, None]
    row_one = 1.0 - BETA_ONE**row_float
    row_two = 1.0 - BETA_TWO**row_float
    expert_first_new, expert_second_new = moments(0, expert_first, expert_second)
    embed_first_new, embed_second_new = moments(1, embed_first, embed_second)
    small_first_new, small_second_new = moments(2, small_first, small_second)
    expert_master_new, expert_update = finish(
        expert_first_new, expert_second_new, expert_master, fixed_one, fixed_two
    )
    embed_master_new, embed_update = finish(
        embed_first_new, embed_second_new, embed_master, row_one, row_two
    )
    small_master_new, small_update = finish(
        small_first_new, small_second_new, small_master, fixed_one, fixed_two
    )
    own = jnp.concatenate(
        [
            embed_master_new.astype(jnp.bfloat16),
            pack_expert(expert_master_new.astype(jnp.bfloat16)),
            jnp.pad(small_master_new.astype(jnp.bfloat16), ((0, 4), (0, 119))),
        ],
        axis=0,
    )
    full = spread(own, ZH, ("z",))
    full = spread(full, Y * ZL, NEAR)
    full = spread(full, C, ("c",)).reshape(C, Y, ZL, ZH, 56, 128)
    full = full.transpose(1, 3, 2, 0, 4, 5)
    embed_weights = full[..., :32, :].reshape(4096, 128)
    expert_weights = full[..., 32:48, :].reshape(Y, ZH, ZL, C, 2, 2, 4, 128)
    expert_weights = expert_weights.transpose(4, 0, 1, 2, 3, 6, 5, 7).reshape(2, 512, 256)
    small_weights = full[..., 48:52, :9].reshape(512, 9)
    return (
        expert_weights,
        embed_weights,
        small_weights,
        expert_master_new,
        expert_first_new,
        expert_second_new,
        embed_master_new,
        embed_first_new,
        embed_second_new,
        embed_update,
        small_master_new,
        small_first_new,
        small_second_new,
        clip_factor,
    )


def solution(mesh):
    fine = Mesh(mesh.devices.reshape(Y, ZH, ZL, C, T), ("y", "z", "w", "c", "t"))
    sh = ("y", "z", "w", "c")
    in_specs = (
        P(None, sh, None, None, "t"),
        P(None, sh, None, "t"),
        P(None, sh, None, "t"),
        P(None, sh, "t"),
        P(None, sh, "t"),
        P(None, sh, "t"),
        P(sh, "t"),
        P(sh, "t"),
        P(sh, "t"),
        P(sh, "t"),
        P(sh, "t"),
        P(sh, "t"),
        P(sh),
        P(),
    )
    out_specs = (
        P(None, None, "t"),
        P(None, "t"),
        P(None, "t"),
        P(None, sh, "t"),
        P(None, sh, "t"),
        P(None, sh, "t"),
        P(sh, "t"),
        P(sh, "t"),
        P(sh, "t"),
        P(sh, "t"),
        P(sh, "t"),
        P(sh, "t"),
        P(sh, "t"),
        P(),
    )
    return jax.shard_map(body, mesh=fine, in_specs=in_specs, out_specs=out_specs, check_vma=False)
```

```python
import functools

import jax
import jax.numpy as jnp
from jax import lax
from jax.experimental import pallas as pl
from jax.experimental.pallas import tpu as pltpu
from jax.sharding import Mesh, PartitionSpec as P

STEP = 1000
P_TOT = 3164160

BETA_ONE = 0.9
BETA_TWO = 0.999
LEARN_RATE = 0.001
DECAY_RATE = 0.1
EPSILON = 1e-08

Y, ZH, W, C, T = 4, 8, 2, 2, 4
A = Y * W
NEAR = ("y", "w")
EMB, EXP, ROWS = 32, 16, 56
SMA = EMB + EXP
SWAP = ((0, 1), (1, 0))
F32, BF16 = jnp.float32, jnp.bfloat16


def whole(shape):
    return pl.BlockSpec(shape, lambda *_: (0,) * len(shape))


def low_rows(shape):
    return lax.broadcasted_iota(jnp.int32, shape, len(shape) - 2) < 4


def flip(x):
    return pltpu.roll(x, 4, x.ndim - 2)


def pack_kernel(expert_ref, embed_ref, small_ref, keep_ref, send_ref):
    first_core = lax.axis_index("c") == 0

    def put(index, rows, zero, one):
        keep_ref[index + rows] = jnp.where(first_core, zero, one)
        send_ref[index + rows] = jnp.where(first_core, one, zero)

    small = small_ref[:, 0, :].astype(F32) + small_ref[:, 1, :].astype(F32)
    small = jnp.concatenate([small, jnp.zeros((128 - 9, 128), F32)], axis=0).T
    for z in range(ZH):
        for w in range(W):
            index = (0, w, z)
            base = (z * W + w) * C * EMB
            pair = [
                embed_ref[0, 0, pl.ds(base + c * EMB, EMB), :].astype(F32)
                + embed_ref[1, 0, pl.ds(base + c * EMB, EMB), :].astype(F32)
                for c in range(C)
            ]
            put(index, (slice(0, EMB),), *pair)
            row = (z * W + w) * 8
            for m in range(2):
                tile = expert_ref[0, 0, m, pl.ds(row, 8), :].astype(F32) + expert_ref[
                    1, 0, m, pl.ds(row, 8), :
                ].astype(F32)
                left, right = tile[:, :128], tile[:, 128:]
                upper = low_rows((8, 128))
                put(
                    index,
                    (slice(EMB + 8 * m, EMB + 8 * m + 8),),
                    jnp.where(upper, left, flip(right)),
                    jnp.where(upper, flip(left), right),
                )
            tile = small[row : row + 8]
            put(index, (slice(SMA, ROWS),), tile, flip(tile))


def pack(expert_grads, embed_grads, small_grads):
    out = jax.ShapeDtypeStruct((Y, W, ZH, ROWS, 128), F32)
    spec = pl.BlockSpec((1, W, ZH, ROWS, 128), lambda y: (y, 0, 0, 0, 0))
    return pl.pallas_call(
        pack_kernel,
        grid=(Y,),
        in_specs=[
            pl.BlockSpec((2, 1, 2, 128, 256), lambda y: (0, 0, 0, y, 0)),
            pl.BlockSpec((2, 1, 1024, 128), lambda y: (0, 0, y, 0)),
            pl.BlockSpec((9, 2, 128), lambda y: (0, 0, y)),
        ],
        out_specs=[spec, spec],
        out_shape=[out, out],
        name="pack",
    )(expert_grads, embed_grads, small_grads[:, 0].transpose(2, 0, 1))


def pair_kernel(keep_ref, got_ref, out_ref):
    out_ref[:, :, :SMA] = (keep_ref[:, :, :SMA] + got_ref[:, :, :SMA]).astype(BF16)
    small = keep_ref[:, :, SMA:] + got_ref[:, :, SMA:]
    high = small.astype(BF16).astype(F32)
    low = small - high
    shape = (W * ZH, 8, 128)
    both = jnp.where(low_rows(shape), high.reshape(shape), flip(low.reshape(shape)))
    out_ref[:, :, SMA:] = both.astype(BF16).reshape(W, ZH, 8, 128)


def add_pair(keep, got):
    spec = pl.BlockSpec((W, ZH, ROWS, 128), lambda y: (y, 0, 0, 0))
    return pl.pallas_call(
        pair_kernel,
        grid=(Y,),
        in_specs=[spec, spec],
        out_specs=spec,
        out_shape=jax.ShapeDtypeStruct((A, ZH, ROWS, 128), BF16),
        name="add_pair",
    )(keep.reshape(A, ZH, ROWS, 128), got.reshape(A, ZH, ROWS, 128))


def near_kernel(got_ref, out_ref):
    total = got_ref[0].astype(F32)
    for a in range(1, A):
        total = total + got_ref[a].astype(F32)
    out_ref[:, :SMA] = total[:, :SMA]
    small = total[:, SMA:]
    out_ref[:, SMA:] = small + flip(small)


def add_near(got):
    return pl.pallas_call(
        near_kernel,
        grid=(4,),
        in_specs=[pl.BlockSpec((A, ZH // 4, ROWS, 128), lambda i: (0, i, 0, 0))],
        out_specs=pl.BlockSpec((ZH // 4, ROWS, 128), lambda i: (i, 0, 0)),
        out_shape=jax.ShapeDtypeStruct((ZH, ROWS, 128), F32),
        name="add_near",
    )(got)


def far_kernel(got_ref, total_ref, line_ref):
    total = got_ref[0]
    for a in range(1, ZH):
        total = total + got_ref[a]
    total_ref[...] = total
    main = total[: SMA + 4]
    line_ref[...] = jnp.full(line_ref.shape, jnp.sum(main * main), F32)


def add_far(got):
    return pl.pallas_call(
        far_kernel,
        out_shape=[
            jax.ShapeDtypeStruct((ROWS, 128), F32),
            jax.ShapeDtypeStruct((A * C * T, 128), F32),
        ],
        name="add_far",
    )(got)


def line_kernel(line_ref, out_ref):
    total = jnp.sum(line_ref[...], axis=0, keepdims=True)
    out_ref[...] = jnp.broadcast_to(total, out_ref.shape)


def add_line(line):
    return pl.pallas_call(
        line_kernel, out_shape=jax.ShapeDtypeStruct((ZH, 128), F32), name="add_line"
    )(line)


def update(scaled, first, second, master, corr_one, corr_two):
    first_new = BETA_ONE * first + (1.0 - BETA_ONE) * scaled
    second_new = BETA_TWO * second + (1.0 - BETA_TWO) * scaled * scaled
    step = (
        first_new / corr_one / (jnp.sqrt(second_new / corr_two) + EPSILON) + DECAY_RATE * master
    )
    return first_new, second_new, step, master - LEARN_RATE * step


def adam_kernel(
    line_ref,
    total_ref,
    rms_ref,
    corr_ref,
    exp_m,
    exp_f,
    exp_s,
    emb_m,
    emb_f,
    emb_s,
    sma_m,
    sma_f,
    sma_s,
    weights_ref,
    exp_mo,
    exp_fo,
    exp_so,
    emb_mo,
    emb_fo,
    emb_so,
    emb_step,
    sma_mo,
    sma_fo,
    sma_so,
    clip_ref,
):
    fixed = (1.0 - BETA_ONE**STEP, 1.0 - BETA_TWO**STEP)
    squares = jnp.sum(line_ref[...], axis=0, keepdims=True)
    factor = rms_ref[0, 0] * jnp.sqrt(P_TOT / squares)
    clip_ref[...] = factor
    first, second, step, master = update(
        factor * total_ref[:EMB], emb_f[...], emb_s[...], emb_m[...], corr_ref[0], corr_ref[1]
    )
    emb_fo[...], emb_so[...], emb_step[...], emb_mo[...] = first, second, step, master
    chunks = [master.astype(BF16).astype(F32)]
    for m in range(2):
        halves = []
        for h in range(2):
            at = (m, slice(None), slice(128 * h, 128 * h + 128))
            row = EMB + 8 * m + 4 * h
            first, second, _, master = update(
                factor * total_ref[row : row + 4], exp_f[at], exp_s[at], exp_m[at], *fixed
            )
            exp_fo[at], exp_so[at], exp_mo[at] = first, second, master
            halves.append(master)
        chunks.append(jnp.concatenate(halves, axis=0))
    first, second, _, master = update(
        factor[:, :9] * total_ref[SMA : SMA + 4, :9], sma_f[...], sma_s[...], sma_m[...], *fixed
    )
    sma_fo[...], sma_so[...], sma_mo[...] = first, second, master
    wide = jnp.concatenate([master, jnp.zeros((4, 128 - 9), F32)], axis=1)
    chunks.append(jnp.concatenate([wide, jnp.zeros((4, 128), F32)], axis=0))
    chunk = jnp.concatenate(chunks, axis=0).astype(BF16)
    for a in range(ZH):
        weights_ref[a] = chunk


def adam(line, total, rms, corr, states):
    shapes = [(ZH, ROWS, 128)] + [(2, 4, 256)] * 3 + [(32, 128)] * 4 + [(4, 9)] * 3 + [(1, 128)]
    out = [jax.ShapeDtypeStruct(n, F32) for n in shapes]
    out[0] = jax.ShapeDtypeStruct(shapes[0], BF16)
    vmem = pl.BlockSpec(memory_space=pltpu.VMEM)
    return pl.pallas_call(
        adam_kernel,
        in_specs=[vmem, vmem, pl.BlockSpec(memory_space=pltpu.SMEM)] + [vmem] * 10,
        out_shape=out,
        name="adam",
    )(line, total, rms, corr, *states)


def unpack_kernel(own_ref, other_ref, expert_ref, embed_ref, small_ref):
    first_core = lax.axis_index("c") == 0
    tiles = []
    for z in range(ZH):
        for w in range(W):
            own, other = own_ref[w, z], other_ref[w, z]
            pair = (jnp.where(first_core, own, other), jnp.where(first_core, other, own))
            base = (z * W + w) * C * EMB
            for c in range(C):
                embed_ref[pl.ds(base + c * EMB, EMB), :] = pair[c][:EMB]
            row = (z * W + w) * 8
            upper = low_rows((8, 128))
            for m in range(2):
                zero, one = (p[EMB + 8 * m : EMB + 8 * m + 8].astype(F32) for p in pair)
                expert_ref[m, pl.ds(row, 8), :128] = jnp.where(upper, zero, flip(one)).astype(BF16)
                expert_ref[m, pl.ds(row, 8), 128:] = jnp.where(upper, flip(zero), one).astype(BF16)
            zero, one = (p[SMA:].astype(F32) for p in pair)
            tiles.append(jnp.where(upper, zero, flip(one)))
    small_ref[...] = jnp.concatenate(tiles, axis=0).T[:9].astype(BF16)


def unpack(own, other):
    spec = pl.BlockSpec((W, ZH, ROWS, 128), lambda y: (y, 0, 0, 0))
    expert, embed, small = pl.pallas_call(
        unpack_kernel,
        grid=(Y,),
        in_specs=[spec, spec],
        out_specs=[
            pl.BlockSpec((2, 128, 256), lambda y: (0, y, 0)),
            pl.BlockSpec((1024, 128), lambda y: (y, 0)),
            pl.BlockSpec((9, 128), lambda y: (0, y)),
        ],
        out_shape=[
            jax.ShapeDtypeStruct((2, 512, 256), BF16),
            jax.ShapeDtypeStruct((4096, 128), BF16),
            jax.ShapeDtypeStruct((9, 512), BF16),
        ],
        name="unpack",
    )(own, other)
    return expert, embed, small.T


def exchange(x, axes):
    return lax.all_to_all(x, axes, 0, 0, tiled=True)


def body(
    expert_grads,
    embed_grads,
    small_grads,
    expert_master,
    expert_first,
    expert_second,
    embed_master,
    embed_first,
    embed_second,
    small_master,
    small_first,
    small_second,
    class_steps,
    clip_rms,
):
    keep, send = pack(expert_grads, embed_grads, small_grads)
    near = add_pair(keep, lax.ppermute(send, "c", SWAP))
    far = add_near(exchange(near, NEAR))
    total, line = add_far(exchange(far, ("z",)))
    line = exchange(add_line(exchange(line, NEAR + ("c", "t"))), ("z",))
    row_float = class_steps.astype(F32)[:, None]
    corr = jnp.stack([1.0 - BETA_ONE**row_float, 1.0 - BETA_TWO**row_float])
    corr = jnp.broadcast_to(corr, (2, EMB, 128))
    states = (
        expert_master,
        expert_first,
        expert_second,
        embed_master,
        embed_first,
        embed_second,
        small_master,
        small_first,
        small_second,
    )
    weights, *new, clip = adam(line, total, clip_rms.reshape(1, 1), corr, states)
    own = exchange(weights, ("z",))
    own = exchange(jnp.broadcast_to(own[None], (A,) + own.shape), NEAR)
    expert_w, embed_w, small_w = unpack(own, lax.ppermute(own, "c", SWAP))
    return (expert_w, embed_w, small_w, *new, clip[0, 0])


def solution(mesh):
    fine = Mesh(mesh.devices.reshape(Y, ZH, W, C, T), ("y", "z", "w", "c", "t"))
    sh = ("y", "z", "w", "c")
    in_specs = (
        P(None, sh, None, None, "t"),
        P(None, sh, None, "t"),
        P(None, sh, None, "t"),
        P(None, sh, "t"),
        P(None, sh, "t"),
        P(None, sh, "t"),
        P(sh, "t"),
        P(sh, "t"),
        P(sh, "t"),
        P(sh, "t"),
        P(sh, "t"),
        P(sh, "t"),
        P(sh),
        P(),
    )
    out_specs = (
        P(None, None, "t"),
        P(None, "t"),
        P(None, "t"),
        P(None, sh, "t"),
        P(None, sh, "t"),
        P(None, sh, "t"),
        P(sh, "t"),
        P(sh, "t"),
        P(sh, "t"),
        P(sh, "t"),
        P(sh, "t"),
        P(sh, "t"),
        P(sh, "t"),
        P(),
    )
    return jax.shard_map(body, mesh=fine, in_specs=in_specs, out_specs=out_specs, check_vma=False)
```

```python
import jax
import jax.numpy as jnp
from jax import lax
from jax.experimental import pallas as pl
from jax.experimental.pallas import tpu as pltpu
from jax.sharding import Mesh, PartitionSpec as P

STEP = 1000
P_TOT = 3164160

BETA_ONE = 0.9
BETA_TWO = 0.999
LEARN_RATE = 0.001
DECAY_RATE = 0.1
EPSILON = 1e-08

Y, ZH, W, C, T = 4, 8, 2, 2, 4
A = Y * W
NEAR = ("y", "w")
EMB, EXP, ROWS = 32, 16, 56
SMA = EMB + EXP
SWAP = ((0, 1), (1, 0))
F32, BF16 = jnp.float32, jnp.bfloat16
VMEM = pl.BlockSpec(memory_space=pltpu.VMEM)


def in_hbm(x):
    return pltpu.with_memory_space_constraint(x, pltpu.HBM)


def low_rows(shape):
    return lax.broadcasted_iota(jnp.int32, shape, len(shape) - 2) < 4


def flip(x):
    return pltpu.roll(x, 4, x.ndim - 2)


def pack_kernel(expert_ref, embed_ref, small_ref, keep_ref, send_ref):
    @pl.when(lax.axis_index("c") == 0)
    def _():
        pack_rows(expert_ref, embed_ref, small_ref, (keep_ref, send_ref))

    @pl.when(lax.axis_index("c") == 1)
    def _():
        pack_rows(expert_ref, embed_ref, small_ref, (send_ref, keep_ref))


def pack_rows(expert_ref, embed_ref, small_ref, outs):
    y = pl.program_id(0)

    def put(index, rows, *values):
        for ref, value in zip(outs, values):
            ref[index + rows] = value

    small = small_ref[:, 0, :].astype(F32) + small_ref[:, 1, :].astype(F32)
    small = jnp.concatenate([small, jnp.zeros((128 - 9, 128), F32)], axis=0).T
    for z in range(ZH):
        for w in range(W):
            index = (y, w, z)
            base = (z * W + w) * C * EMB
            pair = [
                embed_ref[0, 0, pl.ds(base + c * EMB, EMB), :].astype(F32)
                + embed_ref[1, 0, pl.ds(base + c * EMB, EMB), :].astype(F32)
                for c in range(C)
            ]
            put(index, (slice(0, EMB),), *pair)
            row = (z * W + w) * 8
            for m in range(2):
                tile = expert_ref[0, 0, m, pl.ds(row, 8), :].astype(F32) + expert_ref[
                    1, 0, m, pl.ds(row, 8), :
                ].astype(F32)
                left, right = tile[:, :128], tile[:, 128:]
                upper = low_rows((8, 128))
                put(
                    index,
                    (slice(EMB + 8 * m, EMB + 8 * m + 8),),
                    jnp.where(upper, left, flip(right)),
                    jnp.where(upper, flip(left), right),
                )
            tile = small[row : row + 8]
            put(index, (slice(SMA, ROWS),), tile, flip(tile))


def pack(expert_grads, embed_grads, small_grads):
    out = pltpu.VMEM((Y, W, ZH, ROWS, 128), F32)
    return pl.pallas_call(
        pack_kernel,
        grid=(Y,),
        in_specs=[
            pl.BlockSpec((2, 1, 2, 128, 256), lambda y: (0, 0, 0, y, 0)),
            pl.BlockSpec((2, 1, 1024, 128), lambda y: (0, 0, y, 0)),
            pl.BlockSpec((9, 2, 128), lambda y: (0, 0, y)),
        ],
        out_specs=[VMEM, VMEM],
        out_shape=[out, out],
        compiler_params=pltpu.CompilerParams(vmem_limit_bytes=16 << 20),
        name="pack",
    )(in_hbm(expert_grads), in_hbm(embed_grads), in_hbm(small_grads[:, 0].transpose(2, 0, 1)))


def add_pair(keep, got):
    part = (keep + got).reshape(A, ZH, ROWS, 128)
    small = part[:, :, SMA : SMA + 4]
    high = lax.reduce_precision(small, 8, 7)
    terms = [part[:, :, :SMA], high, small - high]
    return jnp.concatenate([x.astype(BF16) for x in terms], axis=2)


def add_near(got):
    total = jnp.sum(got.astype(F32), axis=0)
    small = total[:, SMA : SMA + 4] + total[:, SMA + 4 :]
    return jnp.concatenate([total[:, :SMA], small, jnp.zeros((ZH, 4, 128), F32)], axis=1)


def update(scaled, first, second, master, corr_one, corr_two):
    first_new = BETA_ONE * first + (1.0 - BETA_ONE) * scaled
    second_new = BETA_TWO * second + (1.0 - BETA_TWO) * scaled * scaled
    step = (
        first_new / corr_one / (jnp.sqrt(second_new / corr_two) + EPSILON) + DECAY_RATE * master
    )
    return first_new, second_new, step, master - LEARN_RATE * step


def adam_kernel(
    line_ref,
    total_ref,
    rms_ref,
    corr_ref,
    exp_m,
    exp_f,
    exp_s,
    emb_m,
    emb_f,
    emb_s,
    sma_m,
    sma_f,
    sma_s,
    weights_ref,
    exp_mo,
    exp_fo,
    exp_so,
    emb_mo,
    emb_fo,
    emb_so,
    emb_step,
    sma_mo,
    sma_fo,
    sma_so,
    clip_ref,
):
    fixed = (1.0 - BETA_ONE**STEP, 1.0 - BETA_TWO**STEP)
    squares = jnp.sum(line_ref[...], axis=0, keepdims=True)
    factor = rms_ref[0, 0] * jnp.sqrt(P_TOT / squares)
    clip_ref[...] = factor
    first, second, step, master = update(
        factor * total_ref[:EMB], emb_f[...], emb_s[...], emb_m[...], corr_ref[0], corr_ref[1]
    )
    emb_fo[...], emb_so[...], emb_step[...], emb_mo[...] = first, second, step, master
    chunks = [master.astype(BF16).astype(F32)]
    for m in range(2):
        halves = []
        for h in range(2):
            at = (m, slice(None), slice(128 * h, 128 * h + 128))
            row = EMB + 8 * m + 4 * h
            first, second, _, master = update(
                factor * total_ref[row : row + 4], exp_f[at], exp_s[at], exp_m[at], *fixed
            )
            exp_fo[at], exp_so[at], exp_mo[at] = first, second, master
            halves.append(master)
        chunks.append(jnp.concatenate(halves, axis=0))
    first, second, _, master = update(
        factor[:, :9] * total_ref[SMA : SMA + 4, :9], sma_f[...], sma_s[...], sma_m[...], *fixed
    )
    sma_fo[...], sma_so[...], sma_mo[...] = first, second, master
    wide = jnp.concatenate([master, jnp.zeros((4, 128 - 9), F32)], axis=1)
    chunks.append(jnp.concatenate([wide, jnp.zeros((4, 128), F32)], axis=0))
    chunk = jnp.concatenate(chunks, axis=0).astype(BF16)
    for a in range(ZH):
        weights_ref[a] = chunk


def adam(line, total, rms, corr, states):
    shapes = [(ZH, ROWS, 128)] + [(2, 4, 256)] * 3 + [(32, 128)] * 4 + [(4, 9)] * 3 + [(1, 128)]
    out = [jax.ShapeDtypeStruct(n, F32) for n in shapes]
    out[0] = pltpu.VMEM(shapes[0], BF16)
    return pl.pallas_call(
        adam_kernel,
        in_specs=[VMEM, VMEM, pl.BlockSpec(memory_space=pltpu.SMEM)] + [VMEM] * 10,
        out_specs=[VMEM] * len(out),
        out_shape=out,
        compiler_params=pltpu.CompilerParams(vmem_limit_bytes=16 << 20),
        name="adam",
    )(line, total, rms, corr, *states)


def unpack_kernel(own_ref, other_ref, expert_ref, embed_ref, small_ref):
    first_core = lax.axis_index("c") == 0
    y = pl.program_id(0)
    tiles = []
    for z in range(ZH):
        for w in range(W):
            own, other = own_ref[y * W + w, z], other_ref[y * W + w, z]
            pair = (jnp.where(first_core, own, other), jnp.where(first_core, other, own))
            base = (z * W + w) * C * EMB
            for c in range(C):
                embed_ref[pl.ds(base + c * EMB, EMB), :] = pair[c][:EMB]
            row = (z * W + w) * 8
            upper = low_rows((8, 128))
            for m in range(2):
                zero, one = (p[EMB + 8 * m : EMB + 8 * m + 8].astype(F32) for p in pair)
                expert_ref[m, pl.ds(row, 8), :128] = jnp.where(upper, zero, flip(one)).astype(BF16)
                expert_ref[m, pl.ds(row, 8), 128:] = jnp.where(upper, flip(zero), one).astype(BF16)
            zero, one = (p[SMA:].astype(F32) for p in pair)
            tiles.append(jnp.where(upper, zero, flip(one)))
    small_ref[...] = jnp.concatenate(tiles, axis=0).T[:9].astype(BF16)


def unpack(own, other):
    expert, embed, small = pl.pallas_call(
        unpack_kernel,
        grid=(Y,),
        in_specs=[VMEM, VMEM],
        out_specs=[
            pl.BlockSpec((2, 128, 256), lambda y: (0, y, 0)),
            pl.BlockSpec((1024, 128), lambda y: (y, 0)),
            pl.BlockSpec((9, 128), lambda y: (0, y)),
        ],
        out_shape=[
            jax.ShapeDtypeStruct((2, 512, 256), BF16),
            jax.ShapeDtypeStruct((4096, 128), BF16),
            jax.ShapeDtypeStruct((9, 512), BF16),
        ],
        compiler_params=pltpu.CompilerParams(vmem_limit_bytes=16 << 20),
        name="unpack",
    )(pltpu.with_memory_space_constraint(own, pltpu.VMEM), pltpu.with_memory_space_constraint(other, pltpu.VMEM))
    return expert, embed, small.T


def exchange(x, axes):
    return lax.all_to_all(x, axes, 0, 0, tiled=True)


def body(
    expert_grads,
    embed_grads,
    small_grads,
    expert_master,
    expert_first,
    expert_second,
    embed_master,
    embed_first,
    embed_second,
    small_master,
    small_first,
    small_second,
    class_steps,
    clip_rms,
):
    row_float = class_steps.astype(F32)[:, None]
    corr = jnp.stack([1.0 - BETA_ONE**row_float, 1.0 - BETA_TWO**row_float])
    corr = jnp.broadcast_to(corr, (2, EMB, 128))
    keep, send = pack(expert_grads, embed_grads, small_grads)
    got, corr = lax.optimization_barrier((lax.ppermute(send, "c", SWAP), corr))
    far = add_near(exchange(add_pair(keep, got), NEAR))
    total = jnp.sum(exchange(far, ("z",)), axis=0)
    squares = jnp.sum(total * total)
    line = exchange(jnp.broadcast_to(squares, (A * C * T, 128)), NEAR + ("c", "t"))
    line = jnp.broadcast_to(jnp.sum(line, axis=0), (ZH, 128))
    line = exchange(line, ("z",))
    states = (
        expert_master,
        expert_first,
        expert_second,
        embed_master,
        embed_first,
        embed_second,
        small_master,
        small_first,
        small_second,
    )
    weights, *new, clip = adam(line, total, clip_rms.reshape(1, 1), corr, states)
    own = exchange(weights, ("z",))
    own = exchange(jnp.broadcast_to(own[None], (A,) + own.shape), NEAR)
    expert_w, embed_w, small_w = unpack(own, lax.ppermute(own, "c", SWAP))
    return (expert_w, embed_w, small_w, *new, clip[0, 0])


def solution(mesh):
    fine = Mesh(mesh.devices.reshape(Y, ZH, W, C, T), ("y", "z", "w", "c", "t"))
    sh = ("y", "z", "w", "c")
    in_specs = (
        P(None, sh, None, None, "t"),
        P(None, sh, None, "t"),
        P(None, sh, None, "t"),
        P(None, sh, "t"),
        P(None, sh, "t"),
        P(None, sh, "t"),
        P(sh, "t"),
        P(sh, "t"),
        P(sh, "t"),
        P(sh, "t"),
        P(sh, "t"),
        P(sh, "t"),
        P(sh),
        P(),
    )
    out_specs = (
        P(None, None, "t"),
        P(None, "t"),
        P(None, "t"),
        P(None, sh, "t"),
        P(None, sh, "t"),
        P(None, sh, "t"),
        P(sh, "t"),
        P(sh, "t"),
        P(sh, "t"),
        P(sh, "t"),
        P(sh, "t"),
        P(sh, "t"),
        P(sh, "t"),
        P(),
    )
    return jax.shard_map(body, mesh=fine, in_specs=in_specs, out_specs=out_specs, check_vma=False)
```

```python
import jax
import jax.numpy as jnp
from jax import lax
from jax.experimental import pallas as pl
from jax.experimental.pallas import tpu as pltpu
from jax.sharding import Mesh, PartitionSpec as P

STEP = 1000
P_TOT = 3164160

BETA_ONE = 0.9
BETA_TWO = 0.999
LEARN_RATE = 0.001
DECAY_RATE = 0.1
EPSILON = 1e-08

Y, ZH, W, C, T = 4, 8, 2, 2, 4
A = Y * W
NEAR = ("y", "w")
EMB, EXP, ROWS = 32, 16, 56
SMA = EMB + EXP
SWAP = ((0, 1), (1, 0))
F32, BF16 = jnp.float32, jnp.bfloat16
VMEM = pl.BlockSpec(memory_space=pltpu.VMEM)


def in_hbm(x):
    return pltpu.with_memory_space_constraint(x, pltpu.HBM)


def low_rows(shape):
    return lax.broadcasted_iota(jnp.int32, shape, len(shape) - 2) < 4


def flip(x):
    return pltpu.roll(x, 4, x.ndim - 2)


def pack_kernel(expert_ref, embed_ref, small_ref, keep_ref, send_ref):
    @pl.when(lax.axis_index("c") == 0)
    def _():
        pack_rows(expert_ref, embed_ref, small_ref, (keep_ref, send_ref))

    @pl.when(lax.axis_index("c") == 1)
    def _():
        pack_rows(expert_ref, embed_ref, small_ref, (send_ref, keep_ref))


def pack_rows(expert_ref, embed_ref, small_ref, outs):
    y = pl.program_id(0)

    def put(index, rows, *values):
        for ref, value in zip(outs, values):
            ref[index + rows] = value

    small = small_ref[:, 0, :].astype(F32) + small_ref[:, 1, :].astype(F32)
    small = jnp.concatenate([small, jnp.zeros((128 - 9, 128), F32)], axis=0).T
    for z in range(ZH):
        for w in range(W):
            index = (y, w, z)
            base = (z * W + w) * C * EMB
            pair = [
                embed_ref[0, 0, pl.ds(base + c * EMB, EMB), :].astype(F32)
                + embed_ref[1, 0, pl.ds(base + c * EMB, EMB), :].astype(F32)
                for c in range(C)
            ]
            put(index, (slice(0, EMB),), *pair)
            row = (z * W + w) * 8
            for m in range(2):
                tile = expert_ref[0, 0, m, pl.ds(row, 8), :].astype(F32) + expert_ref[
                    1, 0, m, pl.ds(row, 8), :
                ].astype(F32)
                left, right = tile[:, :128], tile[:, 128:]
                upper = low_rows((8, 128))
                put(
                    index,
                    (slice(EMB + 8 * m, EMB + 8 * m + 8),),
                    jnp.where(upper, left, flip(right)),
                    jnp.where(upper, flip(left), right),
                )
            tile = small[row : row + 8]
            put(index, (slice(SMA, ROWS),), tile, flip(tile))


def pack(expert_grads, embed_grads, small_grads):
    out = pltpu.VMEM((Y, W, ZH, ROWS, 128), F32)
    return pl.pallas_call(
        pack_kernel,
        grid=(Y,),
        in_specs=[
            pl.BlockSpec((2, 1, 2, 128, 256), lambda y: (0, 0, 0, y, 0)),
            pl.BlockSpec((2, 1, 1024, 128), lambda y: (0, 0, y, 0)),
            pl.BlockSpec((9, 2, 128), lambda y: (0, 0, y)),
        ],
        out_specs=[VMEM, VMEM],
        out_shape=[out, out],
        compiler_params=pltpu.CompilerParams(vmem_limit_bytes=16 << 20),
        name="pack",
    )(in_hbm(expert_grads), in_hbm(embed_grads), in_hbm(small_grads[:, 0].transpose(2, 0, 1)))


def terms(part):
    main, small = part[..., :SMA, :], part[..., SMA : SMA + 4, :]
    high = lax.reduce_precision(small, 8, 7)
    return jnp.concatenate([x.astype(BF16) for x in (main, high, small - high)], axis=-2)


def add_near(got):
    total = jnp.sum(got.astype(F32), axis=0)
    return terms(jnp.concatenate([total[:, :SMA], total[:, SMA : SMA + 4] + total[:, SMA + 4 :]], axis=1))


def far_kernel(got_ref, total_ref, line_ref):
    total = got_ref[0].astype(F32)
    for k in range(1, ZH):
        total = total + got_ref[k].astype(F32)
    small = total[SMA:] + flip(total[SMA:])
    total_ref[:SMA] = total[:SMA]
    total_ref[SMA:] = small
    squares = jnp.sum(total[:SMA] * total[:SMA]) + 0.5 * jnp.sum(small * small)
    line_ref[...] = jnp.full(line_ref.shape, squares, F32)


def add_far(got):
    return pl.pallas_call(
        far_kernel,
        in_specs=[VMEM],
        out_specs=[VMEM, VMEM],
        out_shape=[pltpu.VMEM((ROWS, 128), F32), pltpu.VMEM((A * C * T, 128), F32)],
        compiler_params=pltpu.CompilerParams(vmem_limit_bytes=16 << 20),
        name="add_far",
    )(pltpu.with_memory_space_constraint(got, pltpu.VMEM))


def update(scaled, first, second, master, corr_one, corr_two):
    first_new = BETA_ONE * first + (1.0 - BETA_ONE) * scaled
    second_new = BETA_TWO * second + (1.0 - BETA_TWO) * scaled * scaled
    step = (
        first_new / corr_one / (jnp.sqrt(second_new / corr_two) + EPSILON) + DECAY_RATE * master
    )
    return first_new, second_new, step, master - LEARN_RATE * step


def adam_kernel(
    line_ref,
    total_ref,
    rms_ref,
    corr_ref,
    exp_m,
    exp_f,
    exp_s,
    emb_m,
    emb_f,
    emb_s,
    sma_m,
    sma_f,
    sma_s,
    weights_ref,
    exp_mo,
    exp_fo,
    exp_so,
    emb_mo,
    emb_fo,
    emb_so,
    emb_step,
    sma_mo,
    sma_fo,
    sma_so,
    clip_ref,
):
    fixed = (1.0 - BETA_ONE**STEP, 1.0 - BETA_TWO**STEP)
    squares = jnp.sum(line_ref[...], axis=0, keepdims=True)
    factor = rms_ref[0, 0] * jnp.sqrt(P_TOT / squares)
    clip_ref[...] = factor
    first, second, step, master = update(
        factor * total_ref[:EMB], emb_f[...], emb_s[...], emb_m[...], corr_ref[0], corr_ref[1]
    )
    emb_fo[...], emb_so[...], emb_step[...], emb_mo[...] = first, second, step, master
    chunks = [master.astype(BF16).astype(F32)]
    for m in range(2):
        halves = []
        for h in range(2):
            at = (m, slice(None), slice(128 * h, 128 * h + 128))
            row = EMB + 8 * m + 4 * h
            first, second, _, master = update(
                factor * total_ref[row : row + 4], exp_f[at], exp_s[at], exp_m[at], *fixed
            )
            exp_fo[at], exp_so[at], exp_mo[at] = first, second, master
            halves.append(master)
        chunks.append(jnp.concatenate(halves, axis=0))
    first, second, _, master = update(
        factor[:, :9] * total_ref[SMA : SMA + 4, :9], sma_f[...], sma_s[...], sma_m[...], *fixed
    )
    sma_fo[...], sma_so[...], sma_mo[...] = first, second, master
    wide = jnp.concatenate([master, jnp.zeros((4, 128 - 9), F32)], axis=1)
    chunks.append(jnp.concatenate([wide, jnp.zeros((4, 128), F32)], axis=0))
    chunk = jnp.concatenate(chunks, axis=0).astype(BF16)
    for a in range(ZH):
        weights_ref[a] = chunk


def adam(line, total, rms, corr, states):
    shapes = [(ZH, ROWS, 128)] + [(2, 4, 256)] * 3 + [(32, 128)] * 4 + [(4, 9)] * 3 + [(1, 128)]
    out = [jax.ShapeDtypeStruct(n, F32) for n in shapes]
    out[0] = pltpu.VMEM(shapes[0], BF16)
    return pl.pallas_call(
        adam_kernel,
        in_specs=[VMEM, VMEM, pl.BlockSpec(memory_space=pltpu.SMEM)] + [VMEM] * 10,
        out_specs=[VMEM] * len(out),
        out_shape=out,
        compiler_params=pltpu.CompilerParams(vmem_limit_bytes=16 << 20),
        name="adam",
    )(line, total, rms, corr, *states)


def unpack_kernel(own_ref, other_ref, expert_ref, embed_ref, small_ref):
    first_core = lax.axis_index("c") == 0
    y = pl.program_id(0)
    tiles = []
    for z in range(ZH):
        for w in range(W):
            own, other = own_ref[y * W + w, z], other_ref[y * W + w, z]
            pair = (jnp.where(first_core, own, other), jnp.where(first_core, other, own))
            base = (z * W + w) * C * EMB
            for c in range(C):
                embed_ref[pl.ds(base + c * EMB, EMB), :] = pair[c][:EMB]
            row = (z * W + w) * 8
            upper = low_rows((8, 128))
            for m in range(2):
                zero, one = (p[EMB + 8 * m : EMB + 8 * m + 8].astype(F32) for p in pair)
                expert_ref[m, pl.ds(row, 8), :128] = jnp.where(upper, zero, flip(one)).astype(BF16)
                expert_ref[m, pl.ds(row, 8), 128:] = jnp.where(upper, flip(zero), one).astype(BF16)
            zero, one = (p[SMA:].astype(F32) for p in pair)
            tiles.append(jnp.where(upper, zero, flip(one)))
    small_ref[...] = jnp.concatenate(tiles, axis=0).T[:9].astype(BF16)


def unpack(own, other):
    expert, embed, small = pl.pallas_call(
        unpack_kernel,
        grid=(Y,),
        in_specs=[VMEM, VMEM],
        out_specs=[
            pl.BlockSpec((2, 128, 256), lambda y: (0, y, 0)),
            pl.BlockSpec((1024, 128), lambda y: (y, 0)),
            pl.BlockSpec((9, 128), lambda y: (0, y)),
        ],
        out_shape=[
            jax.ShapeDtypeStruct((2, 512, 256), BF16),
            jax.ShapeDtypeStruct((4096, 128), BF16),
            jax.ShapeDtypeStruct((9, 512), BF16),
        ],
        compiler_params=pltpu.CompilerParams(vmem_limit_bytes=16 << 20),
        name="unpack",
    )(pltpu.with_memory_space_constraint(own, pltpu.VMEM), pltpu.with_memory_space_constraint(other, pltpu.VMEM))
    return expert, embed, small.T


def exchange(x, axes):
    return lax.all_to_all(x, axes, 0, 0, tiled=True)


def body(
    expert_grads,
    embed_grads,
    small_grads,
    expert_master,
    expert_first,
    expert_second,
    embed_master,
    embed_first,
    embed_second,
    small_master,
    small_first,
    small_second,
    class_steps,
    clip_rms,
):
    row_float = class_steps.astype(F32)[:, None]
    corr = jnp.stack([1.0 - BETA_ONE**row_float, 1.0 - BETA_TWO**row_float])
    corr = jnp.broadcast_to(corr, (2, EMB, 128))
    keep, send = pack(expert_grads, embed_grads, small_grads)
    got, corr = lax.optimization_barrier((lax.ppermute(send, "c", SWAP), corr))
    near = terms((keep + got).reshape(A, ZH, ROWS, 128))
    far = add_near(exchange(near, NEAR))
    total, line = add_far(exchange(far, ("z",)))
    line = jnp.sum(exchange(line, NEAR + ("c", "t")), axis=0)
    line = exchange(jnp.broadcast_to(line, (ZH, 128)), ("z",))
    states = (
        expert_master,
        expert_first,
        expert_second,
        embed_master,
        embed_first,
        embed_second,
        small_master,
        small_first,
        small_second,
    )
    weights, *new, clip = adam(line, total, clip_rms.reshape(1, 1), corr, states)
    own = exchange(weights, ("z",))
    own = exchange(jnp.broadcast_to(own[None], (A,) + own.shape), NEAR)
    expert_w, embed_w, small_w = unpack(own, lax.ppermute(own, "c", SWAP))
    return (expert_w, embed_w, small_w, *new, clip[0, 0])


def solution(mesh):
    fine = Mesh(mesh.devices.reshape(Y, ZH, W, C, T), ("y", "z", "w", "c", "t"))
    sh = ("y", "z", "w", "c")
    in_specs = (
        P(None, sh, None, None, "t"),
        P(None, sh, None, "t"),
        P(None, sh, None, "t"),
        P(None, sh, "t"),
        P(None, sh, "t"),
        P(None, sh, "t"),
        P(sh, "t"),
        P(sh, "t"),
        P(sh, "t"),
        P(sh, "t"),
        P(sh, "t"),
        P(sh, "t"),
        P(sh),
        P(),
    )
    out_specs = (
        P(None, None, "t"),
        P(None, "t"),
        P(None, "t"),
        P(None, sh, "t"),
        P(None, sh, "t"),
        P(None, sh, "t"),
        P(sh, "t"),
        P(sh, "t"),
        P(sh, "t"),
        P(sh, "t"),
        P(sh, "t"),
        P(sh, "t"),
        P(sh, "t"),
        P(),
    )
    return jax.shard_map(body, mesh=fine, in_specs=in_specs, out_specs=out_specs, check_vma=False)
```

```python
import jax
import jax.numpy as jnp
from jax import lax
from jax.experimental import pallas as pl
from jax.experimental.pallas import tpu as pltpu
from jax.sharding import Mesh, PartitionSpec as P

STEP = 1000
P_TOT = 3164160

BETA_ONE = 0.9
BETA_TWO = 0.999
LEARN_RATE = 0.001
DECAY_RATE = 0.1
EPSILON = 1e-08

Y, ZH, W, C, T = 4, 8, 2, 2, 4
A = Y * W
NEAR = ("y", "w")
EMB, EXP, ROWS = 32, 16, 56
SMA = EMB + EXP
SWAP = ((0, 1), (1, 0))
F32, BF16 = jnp.float32, jnp.bfloat16
VMEM = pl.BlockSpec(memory_space=pltpu.VMEM)


def in_hbm(x):
    return pltpu.with_memory_space_constraint(x, pltpu.HBM)


def in_vmem(x):
    return pltpu.with_memory_space_constraint(x, pltpu.VMEM)


def low_rows(shape):
    return lax.broadcasted_iota(jnp.int32, shape, len(shape) - 2) < 4


def flip(x):
    return pltpu.roll(x, 4, x.ndim - 2)


def two_terms(x):
    high = x.astype(BF16).astype(F32)
    return jnp.where(low_rows(x.shape), high, flip(x - high))


def pack_kernel(expert_hbm, embed_hbm, small_hbm, keep_ref, send_ref, expert, embed, small, sems):
    def copies(y):
        rows = embed_hbm.at[:, 0, pl.ds(y * 1024, 1024)]
        tiles = expert_hbm.at[:, 0, :, pl.ds(y * 128, 128)]
        lanes = small_hbm.at[:, :, pl.ds(y * 128, 128)]
        return [
            pltpu.make_async_copy(rows, embed.at[y], sems.at[0, y]),
            pltpu.make_async_copy(tiles, expert.at[y], sems.at[1, y]),
            pltpu.make_async_copy(lanes, small.at[y], sems.at[2, y]),
        ]

    for y in range(Y):
        for copy in copies(y):
            copy.start()

    @pl.loop(0, Y)
    def _(y):
        for copy in copies(y):
            copy.wait()
        for core in range(C):

            @pl.when(lax.axis_index("c") == core)
            def _():
                pack_rows(core, y, expert, embed, small, keep_ref, send_ref)


def pack_rows(core, y, expert_ref, embed_ref, small_ref, keep_ref, send_ref):
    def put(index, rows, *values):
        keep_ref[index + rows] = values[core]
        send_ref[index + rows] = values[1 - core].astype(BF16)

    small = small_ref[y, :, 0, :].astype(F32) + small_ref[y, :, 1, :].astype(F32)
    small = jnp.concatenate([small, jnp.zeros((128 - 9, 128), F32)], axis=0).T
    for z in range(ZH):
        for w in range(W):
            index = (y * W + w, z)
            base = (z * W + w) * C * EMB
            pair = [
                embed_ref[y, 0, pl.ds(base + c * EMB, EMB), :].astype(F32)
                + embed_ref[y, 1, pl.ds(base + c * EMB, EMB), :].astype(F32)
                for c in range(C)
            ]
            put(index, (slice(0, EMB),), *pair)
            row = (z * W + w) * 8
            for m in range(2):
                tile = expert_ref[y, 0, m, pl.ds(row, 8), :].astype(F32) + expert_ref[
                    y, 1, m, pl.ds(row, 8), :
                ].astype(F32)
                left, right = tile[:, :128], tile[:, 128:]
                upper = low_rows((8, 128))
                put(
                    index,
                    (slice(EMB + 8 * m, EMB + 8 * m + 8),),
                    jnp.where(upper, left, flip(right)),
                    jnp.where(upper, flip(left), right),
                )
            pair = [small[row : row + 8], flip(small[row : row + 8])]
            pair[1 - core] = two_terms(pair[1 - core])
            put(index, (slice(SMA, ROWS),), *pair)


def pack(expert_grads, embed_grads, small_grads):
    shape = (A, ZH, ROWS, 128)
    return pl.pallas_call(
        pack_kernel,
        in_specs=[pl.BlockSpec(memory_space=pltpu.HBM)] * 3,
        out_specs=[VMEM, VMEM],
        out_shape=[pltpu.VMEM(shape, F32), pltpu.VMEM(shape, BF16)],
        scratch_shapes=[
            pltpu.VMEM((Y, 2, 2, 128, 256), BF16),
            pltpu.VMEM((Y, 2, 1024, 128), BF16),
            pltpu.VMEM((Y, 9, 2, 128), BF16),
            pltpu.SemaphoreType.DMA((3, Y)),
        ],
        compiler_params=pltpu.CompilerParams(vmem_limit_bytes=16 << 20),
        name="pack",
    )(in_hbm(expert_grads), in_hbm(embed_grads), in_hbm(small_grads[:, 0].transpose(2, 0, 1)))


def terms(main, small):
    high = lax.reduce_precision(small, 8, 7)
    return jnp.concatenate([x.astype(BF16) for x in (main, high, small - high)], axis=-2)


def parts(x):
    x = x.astype(F32)
    return x[..., :SMA, :], x[..., SMA : SMA + 4, :] + x[..., SMA + 4 :, :]


def pair_kernel(keep_ref, got_ref, out_ref):
    @pl.loop(0, A)
    def _(a):
        out_ref[a, :, :SMA] = (keep_ref[a, :, :SMA] + got_ref[a, :, :SMA].astype(F32)).astype(BF16)
        small = got_ref[a, :, SMA:].astype(F32)
        small = keep_ref[a, :, SMA:] + (small + flip(small))
        out_ref[a, :, SMA:] = two_terms(small).astype(BF16)


def add_pair(keep, got):
    return pl.pallas_call(
        pair_kernel,
        in_specs=[VMEM, VMEM],
        out_specs=VMEM,
        out_shape=pltpu.VMEM((A, ZH, ROWS, 128), BF16),
        compiler_params=pltpu.CompilerParams(vmem_limit_bytes=16 << 20),
        name="add_pair",
    )(in_vmem(keep), in_vmem(got))


def add_near(got):
    return terms(*parts(jnp.sum(got.astype(F32), axis=0)))


def far_kernel(got_ref, total_ref, line_ref):
    total = got_ref[0].astype(F32)
    for k in range(1, ZH):
        total = total + got_ref[k].astype(F32)
    small = total[SMA:] + flip(total[SMA:])
    total_ref[:SMA] = total[:SMA]
    total_ref[SMA:] = small
    squares = jnp.sum(total[:SMA] * total[:SMA]) + 0.5 * jnp.sum(small * small)
    line_ref[...] = jnp.full(line_ref.shape, squares, F32)


def add_far(got):
    return pl.pallas_call(
        far_kernel,
        in_specs=[VMEM],
        out_specs=[VMEM, VMEM],
        out_shape=[pltpu.VMEM((ROWS, 128), F32), pltpu.VMEM((A * C * T, 128), F32)],
        compiler_params=pltpu.CompilerParams(vmem_limit_bytes=16 << 20),
        name="add_far",
    )(in_vmem(got))


def update(scaled, first, second, master, corr_one, corr_two):
    first_new = BETA_ONE * first + (1.0 - BETA_ONE) * scaled
    second_new = BETA_TWO * second + (1.0 - BETA_TWO) * scaled * scaled
    step = (
        first_new / corr_one / (jnp.sqrt(second_new / corr_two) + EPSILON) + DECAY_RATE * master
    )
    return first_new, second_new, step, master - LEARN_RATE * step


def adam_kernel(
    line_ref,
    total_ref,
    rms_ref,
    corr_ref,
    exp_m,
    exp_f,
    exp_s,
    emb_m,
    emb_f,
    emb_s,
    sma_m,
    sma_f,
    sma_s,
    weights_ref,
    exp_mo,
    exp_fo,
    exp_so,
    emb_mo,
    emb_fo,
    emb_so,
    emb_step,
    sma_mo,
    sma_fo,
    sma_so,
    clip_ref,
):
    fixed = (1.0 - BETA_ONE**STEP, 1.0 - BETA_TWO**STEP)
    squares = jnp.sum(line_ref[...], axis=0, keepdims=True)
    factor = rms_ref[...] * jnp.sqrt(P_TOT / squares)
    clip_ref[...] = factor
    first, second, step, master = update(
        factor * total_ref[:EMB], emb_f[...], emb_s[...], emb_m[...], corr_ref[0], corr_ref[1]
    )
    emb_fo[...], emb_so[...], emb_step[...], emb_mo[...] = first, second, step, master
    chunks = [master.astype(BF16).astype(F32)]
    for m in range(2):
        halves = []
        for h in range(2):
            at = (m, slice(None), slice(128 * h, 128 * h + 128))
            row = EMB + 8 * m + 4 * h
            first, second, _, master = update(
                factor * total_ref[row : row + 4], exp_f[at], exp_s[at], exp_m[at], *fixed
            )
            exp_fo[at], exp_so[at], exp_mo[at] = first, second, master
            halves.append(master)
        chunks.append(jnp.concatenate(halves, axis=0))
    first, second, _, master = update(
        factor[:, :9] * total_ref[SMA : SMA + 4, :9], sma_f[...], sma_s[...], sma_m[...], *fixed
    )
    sma_fo[...], sma_so[...], sma_mo[...] = first, second, master
    wide = jnp.concatenate([master, jnp.zeros((4, 128 - 9), F32)], axis=1)
    chunks.append(jnp.concatenate([wide, jnp.zeros((4, 128), F32)], axis=0))
    chunk = jnp.concatenate(chunks, axis=0).astype(BF16)
    for a in range(ZH):
        weights_ref[a] = chunk


def adam(line, total, rms, corr, states):
    shapes = [(ZH, ROWS, 128)] + [(2, 4, 256)] * 3 + [(32, 128)] * 4 + [(4, 9)] * 3 + [(1, 128)]
    out = [jax.ShapeDtypeStruct(n, F32) for n in shapes]
    out[0] = pltpu.VMEM(shapes[0], BF16)
    return pl.pallas_call(
        adam_kernel,
        in_specs=[VMEM] * 13,
        out_specs=[VMEM] * len(out),
        out_shape=out,
        compiler_params=pltpu.CompilerParams(vmem_limit_bytes=16 << 20),
        name="adam",
    )(line, total, rms, corr, *states)


def unpack_kernel(own_ref, other_ref, expert_ref, embed_ref, small_ref):
    for core in range(C):

        @pl.when(lax.axis_index("c") == core)
        def _():
            pair = (own_ref, other_ref) if core == 0 else (other_ref, own_ref)
            unpack_rows(pair, expert_ref, embed_ref, small_ref)


def unpack_rows(refs, expert_ref, embed_ref, small_ref):
    y = pl.program_id(0)
    tiles = []
    for z in range(ZH):
        for w in range(W):
            pair = [ref[y * W + w, z] for ref in refs]
            base = (z * W + w) * C * EMB
            for c in range(C):
                embed_ref[pl.ds(base + c * EMB, EMB), :] = pair[c][:EMB]
            row = (z * W + w) * 8
            upper = low_rows((8, 128))
            for m in range(2):
                zero, one = (p[EMB + 8 * m : EMB + 8 * m + 8].astype(F32) for p in pair)
                expert_ref[m, pl.ds(row, 8), :128] = jnp.where(upper, zero, flip(one)).astype(BF16)
                expert_ref[m, pl.ds(row, 8), 128:] = jnp.where(upper, flip(zero), one).astype(BF16)
            zero, one = (p[SMA:].astype(F32) for p in pair)
            tiles.append(jnp.where(upper, zero, flip(one)))
    small_ref[...] = jnp.concatenate(tiles, axis=0).T[:9].astype(BF16)


def unpack(own, other):
    expert, embed, small = pl.pallas_call(
        unpack_kernel,
        grid=(Y,),
        in_specs=[VMEM, VMEM],
        out_specs=[
            pl.BlockSpec((2, 128, 256), lambda y: (0, y, 0)),
            pl.BlockSpec((1024, 128), lambda y: (y, 0)),
            pl.BlockSpec((9, 128), lambda y: (0, y)),
        ],
        out_shape=[
            jax.ShapeDtypeStruct((2, 512, 256), BF16),
            jax.ShapeDtypeStruct((4096, 128), BF16),
            jax.ShapeDtypeStruct((9, 512), BF16),
        ],
        compiler_params=pltpu.CompilerParams(vmem_limit_bytes=16 << 20),
        name="unpack",
    )(in_vmem(own), in_vmem(other))
    return expert, embed, small.T


def exchange(x, axes):
    return lax.all_to_all(x, axes, 0, 0, tiled=True)


def body(
    expert_grads,
    embed_grads,
    small_grads,
    expert_master,
    expert_first,
    expert_second,
    embed_master,
    embed_first,
    embed_second,
    small_master,
    small_first,
    small_second,
    class_steps,
    clip_rms,
):
    row_float = class_steps.astype(F32)[:, None]
    corr = jnp.stack([1.0 - BETA_ONE**row_float, 1.0 - BETA_TWO**row_float])
    corr = jnp.broadcast_to(corr, (2, EMB, 128))
    keep, send = pack(expert_grads, embed_grads, small_grads)
    rms = jnp.broadcast_to(clip_rms, (1, 128))
    got, corr, rms = lax.optimization_barrier((lax.ppermute(send, "c", SWAP), corr, rms))
    far = add_near(exchange(add_pair(keep, got), NEAR))
    total, line = add_far(exchange(far, ("z",)))
    line = jnp.sum(exchange(line, NEAR + ("c", "t")), axis=0)
    line = exchange(jnp.broadcast_to(line, (ZH, 128)), ("z",))
    states = (
        expert_master,
        expert_first,
        expert_second,
        embed_master,
        embed_first,
        embed_second,
        small_master,
        small_first,
        small_second,
    )
    weights, *new, clip = adam(line, total, rms, corr, states)
    own = exchange(weights, ("z",))
    own = exchange(jnp.broadcast_to(own[None], (A,) + own.shape), NEAR)
    expert_w, embed_w, small_w = unpack(own, lax.ppermute(own, "c", SWAP))
    return (expert_w, embed_w, small_w, *new, clip[0, 0])


def solution(mesh):
    fine = Mesh(mesh.devices.reshape(Y, ZH, W, C, T), ("y", "z", "w", "c", "t"))
    sh = ("y", "z", "w", "c")
    in_specs = (
        P(None, sh, None, None, "t"),
        P(None, sh, None, "t"),
        P(None, sh, None, "t"),
        P(None, sh, "t"),
        P(None, sh, "t"),
        P(None, sh, "t"),
        P(sh, "t"),
        P(sh, "t"),
        P(sh, "t"),
        P(sh, "t"),
        P(sh, "t"),
        P(sh, "t"),
        P(sh),
        P(),
    )
    out_specs = (
        P(None, None, "t"),
        P(None, "t"),
        P(None, "t"),
        P(None, sh, "t"),
        P(None, sh, "t"),
        P(None, sh, "t"),
        P(sh, "t"),
        P(sh, "t"),
        P(sh, "t"),
        P(sh, "t"),
        P(sh, "t"),
        P(sh, "t"),
        P(sh, "t"),
        P(),
    )
    return jax.shard_map(body, mesh=fine, in_specs=in_specs, out_specs=out_specs, check_vma=False)
```

```python
import jax
import jax.numpy as jnp
from jax import lax
from jax.experimental import pallas as pl
from jax.experimental.pallas import tpu as pltpu
from jax.sharding import Mesh, PartitionSpec as P

STEP = 1000
P_TOT = 3164160

BETA_ONE = 0.9
BETA_TWO = 0.999
LEARN_RATE = 0.001
DECAY_RATE = 0.1
EPSILON = 1e-08

Y, ZH, W, C, T = 4, 8, 2, 2, 4
A = Y * W
NEAR = ("y", "w")
EMB, EXP, ROWS = 32, 16, 56
SMA = EMB + EXP
MAIN, MSG = ZH * SMA, ZH * SMA + 8
SWAP = ((0, 1), (1, 0))
F32, BF16 = jnp.float32, jnp.bfloat16
VMEM = pl.BlockSpec(memory_space=pltpu.VMEM)


def in_hbm(x):
    return pltpu.with_memory_space_constraint(x, pltpu.HBM)


def in_vmem(x):
    return pltpu.with_memory_space_constraint(x, pltpu.VMEM)


def low_rows(shape):
    return lax.broadcasted_iota(jnp.int32, shape, len(shape) - 2) < 4


def flip(x):
    return pltpu.roll(x, 4, x.ndim - 2)


def shift(x, z, back=False):
    return pltpu.roll(x, (128 - 9 * z) % 128 if back else 9 * z, x.ndim - 1)


def nine(x):
    return jnp.where(lax.broadcasted_iota(jnp.int32, x.shape, x.ndim - 1) < 9, x, 0.0)


def two_terms(x):
    high = x.astype(BF16).astype(F32)
    return jnp.where(low_rows(x.shape), high, flip(x - high))


def pack_kernel(expert_hbm, embed_hbm, small_hbm, keep_ref, send_ref, expert, embed, small, sems):
    def copies(y):
        rows = embed_hbm.at[:, 0, pl.ds(y * 1024, 1024)]
        tiles = expert_hbm.at[:, 0, :, pl.ds(y * 128, 128)]
        lanes = small_hbm.at[:, :, pl.ds(y * 128, 128)]
        return [
            pltpu.make_async_copy(rows, embed.at[y], sems.at[0, y]),
            pltpu.make_async_copy(tiles, expert.at[y], sems.at[1, y]),
            pltpu.make_async_copy(lanes, small.at[y], sems.at[2, y]),
        ]

    for y in range(Y):
        for copy in copies(y):
            copy.start()

    @pl.loop(0, Y)
    def _(y):
        for copy in copies(y):
            copy.wait()
        for core in range(C):

            @pl.when(lax.axis_index("c") == core)
            def _():
                pack_rows(core, y, expert, embed, small, keep_ref, send_ref)


def pack_rows(core, y, expert_ref, embed_ref, small_ref, keep_ref, send_ref):
    def put(w, row, rows, *values):
        at = (y * W + w, pl.ds(row, rows))
        keep_ref[at] = values[core]
        send_ref[at] = values[1 - core].astype(BF16)

    small = small_ref[y, :, 0, :].astype(F32) + small_ref[y, :, 1, :].astype(F32)
    small = jnp.concatenate([small, jnp.zeros((128 - 9, 128), F32)], axis=0).T
    for w in range(W):
        shared = jnp.zeros((8, 128), F32)
        for z in range(ZH):
            base = (z * W + w) * C * EMB
            pair = [
                embed_ref[y, 0, pl.ds(base + c * EMB, EMB), :].astype(F32)
                + embed_ref[y, 1, pl.ds(base + c * EMB, EMB), :].astype(F32)
                for c in range(C)
            ]
            put(w, z * SMA, EMB, *pair)
            row = (z * W + w) * 8
            for m in range(2):
                tile = expert_ref[y, 0, m, pl.ds(row, 8), :].astype(F32) + expert_ref[
                    y, 1, m, pl.ds(row, 8), :
                ].astype(F32)
                left, right = tile[:, :128], tile[:, 128:]
                upper = low_rows((8, 128))
                put(
                    w,
                    z * SMA + EMB + 8 * m,
                    8,
                    jnp.where(upper, left, flip(right)),
                    jnp.where(upper, flip(left), right),
                )
            shared = shared + shift(small[row : row + 8], z)
        pair = [shared, flip(shared)]
        pair[1 - core] = two_terms(pair[1 - core])
        put(w, MAIN, 8, *pair)


def pack(expert_grads, embed_grads, small_grads):
    shape = (A, MSG, 128)
    return pl.pallas_call(
        pack_kernel,
        in_specs=[pl.BlockSpec(memory_space=pltpu.HBM)] * 3,
        out_specs=[VMEM, VMEM],
        out_shape=[pltpu.VMEM(shape, F32), pltpu.VMEM(shape, BF16)],
        scratch_shapes=[
            pltpu.VMEM((Y, 2, 2, 128, 256), BF16),
            pltpu.VMEM((Y, 2, 1024, 128), BF16),
            pltpu.VMEM((Y, 9, 2, 128), BF16),
            pltpu.SemaphoreType.DMA((3, Y)),
        ],
        compiler_params=pltpu.CompilerParams(vmem_limit_bytes=16 << 20),
        name="pack",
    )(in_hbm(expert_grads), in_hbm(embed_grads), in_hbm(small_grads[:, 0].transpose(2, 0, 1)))


def kernel_in_vmem(kernel, name, shapes, *args):
    return pl.pallas_call(
        kernel,
        in_specs=[VMEM] * len(args),
        out_specs=[VMEM] * len(shapes),
        out_shape=[pltpu.VMEM(*shape) for shape in shapes],
        compiler_params=pltpu.CompilerParams(vmem_limit_bytes=16 << 20),
        name=name,
    )(*(in_vmem(x) for x in args))


def pair_kernel(keep_ref, got_ref, out_ref):
    @pl.loop(0, A)
    def _(a):
        out_ref[a, :MAIN] = (keep_ref[a, :MAIN] + got_ref[a, :MAIN].astype(F32)).astype(BF16)
        small = got_ref[a, MAIN:].astype(F32)
        small = keep_ref[a, MAIN:] + (small + flip(small))
        out_ref[a, MAIN:] = two_terms(small).astype(BF16)


def add_pair(keep, got):
    return kernel_in_vmem(pair_kernel, "add_pair", [((A, MSG, 128), BF16)], keep, got)[0]


def near_kernel(got_ref, out_ref):
    def total(rows):
        out = got_ref[0, rows].astype(F32)
        for a in range(1, A):
            out = out + got_ref[a, rows].astype(F32)
        return out

    shared = total(slice(MAIN, MSG))
    shared = shared + flip(shared)
    for z in range(ZH):
        out_ref[z, :SMA] = total(slice(z * SMA, z * SMA + SMA)).astype(BF16)
        out_ref[z, SMA:] = two_terms(nine(shift(shared, z, True))).astype(BF16)


def add_near(got):
    return kernel_in_vmem(near_kernel, "add_near", [((ZH, ROWS, 128), BF16)], got)[0]


def spread_kernel(own_ref, out_ref):
    shared = jnp.zeros((8, 128), F32)
    for z in range(ZH):
        main = own_ref[z, :SMA]
        for a in range(A):
            out_ref[a, z * SMA : z * SMA + SMA] = main
        shared = shared + shift(nine(own_ref[z, SMA:].astype(F32)), z)
    for a in range(A):
        out_ref[a, MAIN:] = shared.astype(BF16)


def spread(own):
    return kernel_in_vmem(spread_kernel, "spread", [((A, MSG, 128), BF16)], own)[0]


def far_kernel(got_ref, total_ref, line_ref):
    total = got_ref[0].astype(F32)
    for k in range(1, ZH):
        total = total + got_ref[k].astype(F32)
    small = total[SMA:] + flip(total[SMA:])
    total_ref[:SMA] = total[:SMA]
    total_ref[SMA:] = small
    squares = jnp.sum(total[:SMA] * total[:SMA]) + 0.5 * jnp.sum(small * small)
    line_ref[...] = jnp.full(line_ref.shape, squares, F32)


def add_far(got):
    return kernel_in_vmem(
        far_kernel, "add_far", [((ROWS, 128), F32), ((A * C * T, 128), F32)], got
    )


def update(scaled, first, second, master, corr_one, corr_two):
    first_new = BETA_ONE * first + (1.0 - BETA_ONE) * scaled
    second_new = BETA_TWO * second + (1.0 - BETA_TWO) * scaled * scaled
    step = (
        first_new / corr_one / (jnp.sqrt(second_new / corr_two) + EPSILON) + DECAY_RATE * master
    )
    return first_new, second_new, step, master - LEARN_RATE * step


def adam_kernel(
    line_ref,
    total_ref,
    rms_ref,
    corr_ref,
    exp_m,
    exp_f,
    exp_s,
    emb_m,
    emb_f,
    emb_s,
    sma_m,
    sma_f,
    sma_s,
    weights_ref,
    exp_mo,
    exp_fo,
    exp_so,
    emb_mo,
    emb_fo,
    emb_so,
    emb_step,
    sma_mo,
    sma_fo,
    sma_so,
    clip_ref,
):
    fixed = (1.0 - BETA_ONE**STEP, 1.0 - BETA_TWO**STEP)
    squares = jnp.sum(line_ref[...], axis=0, keepdims=True)
    factor = rms_ref[...] * jnp.sqrt(P_TOT / squares)
    clip_ref[...] = factor
    first, second, step, master = update(
        factor * total_ref[:EMB], emb_f[...], emb_s[...], emb_m[...], corr_ref[0], corr_ref[1]
    )
    emb_fo[...], emb_so[...], emb_step[...], emb_mo[...] = first, second, step, master
    chunks = [master.astype(BF16).astype(F32)]
    for m in range(2):
        halves = []
        for h in range(2):
            at = (m, slice(None), slice(128 * h, 128 * h + 128))
            row = EMB + 8 * m + 4 * h
            first, second, _, master = update(
                factor * total_ref[row : row + 4], exp_f[at], exp_s[at], exp_m[at], *fixed
            )
            exp_fo[at], exp_so[at], exp_mo[at] = first, second, master
            halves.append(master)
        chunks.append(jnp.concatenate(halves, axis=0))
    first, second, _, master = update(
        factor[:, :9] * total_ref[SMA : SMA + 4, :9], sma_f[...], sma_s[...], sma_m[...], *fixed
    )
    sma_fo[...], sma_so[...], sma_mo[...] = first, second, master
    wide = jnp.concatenate([master, jnp.zeros((4, 128 - 9), F32)], axis=1)
    chunks.append(jnp.concatenate([wide, jnp.zeros((4, 128), F32)], axis=0))
    chunk = jnp.concatenate(chunks, axis=0).astype(BF16)
    for a in range(ZH):
        weights_ref[a] = chunk


def adam(line, total, rms, corr, states):
    shapes = [(ZH, ROWS, 128)] + [(2, 4, 256)] * 3 + [(32, 128)] * 4 + [(4, 9)] * 3 + [(1, 128)]
    out = [jax.ShapeDtypeStruct(n, F32) for n in shapes]
    out[0] = pltpu.VMEM(shapes[0], BF16)
    return pl.pallas_call(
        adam_kernel,
        in_specs=[VMEM] * 13,
        out_specs=[VMEM] * len(out),
        out_shape=out,
        compiler_params=pltpu.CompilerParams(vmem_limit_bytes=16 << 20),
        name="adam",
    )(line, total, rms, corr, *states)


def unpack_kernel(own_ref, other_ref, expert_ref, embed_ref, small_ref):
    for core in range(C):

        @pl.when(lax.axis_index("c") == core)
        def _():
            pair = (own_ref, other_ref) if core == 0 else (other_ref, own_ref)
            unpack_rows(pair, expert_ref, embed_ref, small_ref)


def unpack_rows(refs, expert_ref, embed_ref, small_ref):
    y = pl.program_id(0)
    upper = low_rows((8, 128))
    tiles = [None] * (ZH * W)
    for w in range(W):
        shared = [ref[y * W + w, MAIN:].astype(F32) for ref in refs]
        shared = jnp.where(upper, shared[0], flip(shared[1]))
        for z in range(ZH):
            pair = [ref[y * W + w, z * SMA : z * SMA + SMA] for ref in refs]
            base = (z * W + w) * C * EMB
            for c in range(C):
                embed_ref[pl.ds(base + c * EMB, EMB), :] = pair[c][:EMB]
            row = (z * W + w) * 8
            for m in range(2):
                zero, one = (p[EMB + 8 * m : EMB + 8 * m + 8].astype(F32) for p in pair)
                expert_ref[m, pl.ds(row, 8), :128] = jnp.where(upper, zero, flip(one)).astype(BF16)
                expert_ref[m, pl.ds(row, 8), 128:] = jnp.where(upper, flip(zero), one).astype(BF16)
            tiles[z * W + w] = shift(shared, z, True)
    small_ref[...] = jnp.concatenate(tiles, axis=0).T[:9].astype(BF16)


def unpack(own, other):
    expert, embed, small = pl.pallas_call(
        unpack_kernel,
        grid=(Y,),
        in_specs=[VMEM, VMEM],
        out_specs=[
            pl.BlockSpec((2, 128, 256), lambda y: (0, y, 0)),
            pl.BlockSpec((1024, 128), lambda y: (y, 0)),
            pl.BlockSpec((9, 128), lambda y: (0, y)),
        ],
        out_shape=[
            jax.ShapeDtypeStruct((2, 512, 256), BF16),
            jax.ShapeDtypeStruct((4096, 128), BF16),
            jax.ShapeDtypeStruct((9, 512), BF16),
        ],
        compiler_params=pltpu.CompilerParams(vmem_limit_bytes=16 << 20),
        name="unpack",
    )(in_vmem(own), in_vmem(other))
    return expert, embed, small.T


def exchange(x, axes):
    return lax.all_to_all(x, axes, 0, 0, tiled=True)


def body(
    expert_grads,
    embed_grads,
    small_grads,
    expert_master,
    expert_first,
    expert_second,
    embed_master,
    embed_first,
    embed_second,
    small_master,
    small_first,
    small_second,
    class_steps,
    clip_rms,
):
    row_float = class_steps.astype(F32)[:, None]
    corr = jnp.stack([1.0 - BETA_ONE**row_float, 1.0 - BETA_TWO**row_float])
    corr = jnp.broadcast_to(corr, (2, EMB, 128))
    keep, send = pack(expert_grads, embed_grads, small_grads)
    rms = jnp.broadcast_to(clip_rms, (1, 128))
    got, corr, rms = lax.optimization_barrier((lax.ppermute(send, "c", SWAP), corr, rms))
    far = add_near(exchange(add_pair(keep, got), NEAR))
    total, line = add_far(exchange(far, ("z",)))
    line = jnp.sum(exchange(line, NEAR + ("c", "t")), axis=0)
    line = exchange(jnp.broadcast_to(line, (ZH, 128)), ("z",))
    states = (
        expert_master,
        expert_first,
        expert_second,
        embed_master,
        embed_first,
        embed_second,
        small_master,
        small_first,
        small_second,
    )
    weights, *new, clip = adam(line, total, rms, corr, states)
    own = exchange(weights, ("z",))
    own = exchange(spread(own), NEAR)
    expert_w, embed_w, small_w = unpack(own, lax.ppermute(own, "c", SWAP))
    return (expert_w, embed_w, small_w, *new, clip[0, 0])


def solution(mesh):
    fine = Mesh(mesh.devices.reshape(Y, ZH, W, C, T), ("y", "z", "w", "c", "t"))
    sh = ("y", "z", "w", "c")
    in_specs = (
        P(None, sh, None, None, "t"),
        P(None, sh, None, "t"),
        P(None, sh, None, "t"),
        P(None, sh, "t"),
        P(None, sh, "t"),
        P(None, sh, "t"),
        P(sh, "t"),
        P(sh, "t"),
        P(sh, "t"),
        P(sh, "t"),
        P(sh, "t"),
        P(sh, "t"),
        P(sh),
        P(),
    )
    out_specs = (
        P(None, None, "t"),
        P(None, "t"),
        P(None, "t"),
        P(None, sh, "t"),
        P(None, sh, "t"),
        P(None, sh, "t"),
        P(sh, "t"),
        P(sh, "t"),
        P(sh, "t"),
        P(sh, "t"),
        P(sh, "t"),
        P(sh, "t"),
        P(sh, "t"),
        P(),
    )
    return jax.shard_map(body, mesh=fine, in_specs=in_specs, out_specs=out_specs, check_vma=False)
```

```python
import jax
import jax.numpy as jnp
from jax import lax
from jax.experimental import pallas as pl
from jax.experimental.pallas import tpu as pltpu
from jax.sharding import Mesh, PartitionSpec as P

STEP = 1000
P_TOT = 3164160

BETA_ONE = 0.9
BETA_TWO = 0.999
LEARN_RATE = 0.001
DECAY_RATE = 0.1
EPSILON = 1e-08

Y, ZH, W, C, T = 4, 8, 2, 2, 4
A = Y * W
NEAR = ("y", "w")
EMB, EXP, ROWS = 32, 16, 56
SMA = EMB + EXP
MAIN, MSG = ZH * SMA, ZH * SMA + 8
SWAP = ((0, 1), (1, 0))
F32, BF16 = jnp.float32, jnp.bfloat16
VMEM = pl.BlockSpec(memory_space=pltpu.VMEM)


def in_hbm(x):
    return pltpu.with_memory_space_constraint(x, pltpu.HBM)


def in_vmem(x):
    return pltpu.with_memory_space_constraint(x, pltpu.VMEM)


def low_rows(shape):
    return lax.broadcasted_iota(jnp.int32, shape, len(shape) - 2) < 4


def flip(x):
    return pltpu.roll(x, 4, x.ndim - 2)


def shift(x, z, back=False):
    return pltpu.roll(x, (128 - 9 * z) % 128 if back else 9 * z, x.ndim - 1)


def nine(x):
    return jnp.where(lax.broadcasted_iota(jnp.int32, x.shape, x.ndim - 1) < 9, x, 0.0)


def two_terms(x):
    high = x.astype(BF16).astype(F32)
    return jnp.where(low_rows(x.shape), high, flip(x - high))


def pack_kernel(expert_hbm, embed_hbm, small_hbm, keep_ref, send_ref, expert, embed, small, sems):
    def copies(y):
        rows = embed_hbm.at[:, 0, pl.ds(y * 1024, 1024)]
        tiles = expert_hbm.at[:, 0, :, pl.ds(y * 128, 128)]
        lanes = small_hbm.at[:, :, pl.ds(y * 128, 128)]
        return [
            pltpu.make_async_copy(rows, embed.at[y], sems.at[0, y]),
            pltpu.make_async_copy(tiles, expert.at[y], sems.at[1, y]),
            pltpu.make_async_copy(lanes, small.at[y], sems.at[2, y]),
        ]

    for y in range(Y):
        for copy in copies(y):
            copy.start()

    @pl.loop(0, Y)
    def _(y):
        for copy in copies(y):
            copy.wait()
        for core in range(C):

            @pl.when(lax.axis_index("c") == core)
            def _():
                pack_rows(core, y, expert, embed, small, keep_ref, send_ref)


def pack_rows(core, y, expert_ref, embed_ref, small_ref, keep_ref, send_ref):
    def put(w, row, rows, *values):
        at = (y * W + w, pl.ds(row, rows))
        keep_ref[at] = values[core]
        send_ref[at] = values[1 - core].astype(BF16)

    small = small_ref[y, :, 0, :].astype(F32) + small_ref[y, :, 1, :].astype(F32)
    small = jnp.concatenate([small, jnp.zeros((128 - 9, 128), F32)], axis=0).T
    for w in range(W):
        shared = jnp.zeros((8, 128), F32)
        for z in range(ZH):
            base = (z * W + w) * C * EMB
            pair = [
                embed_ref[y, 0, pl.ds(base + c * EMB, EMB), :].astype(F32)
                + embed_ref[y, 1, pl.ds(base + c * EMB, EMB), :].astype(F32)
                for c in range(C)
            ]
            put(w, z * SMA, EMB, *pair)
            row = (z * W + w) * 8
            for m in range(2):
                tile = expert_ref[y, 0, m, pl.ds(row, 8), :].astype(F32) + expert_ref[
                    y, 1, m, pl.ds(row, 8), :
                ].astype(F32)
                left, right = tile[:, :128], tile[:, 128:]
                upper = low_rows((8, 128))
                put(
                    w,
                    z * SMA + EMB + 8 * m,
                    8,
                    jnp.where(upper, left, flip(right)),
                    jnp.where(upper, flip(left), right),
                )
            shared = shared + shift(small[row : row + 8], z)
        pair = [shared, flip(shared)]
        pair[1 - core] = two_terms(pair[1 - core])
        put(w, MAIN, 8, *pair)


def pack(expert_grads, embed_grads, small_grads):
    shape = (A, MSG, 128)
    return pl.pallas_call(
        pack_kernel,
        in_specs=[pl.BlockSpec(memory_space=pltpu.HBM)] * 3,
        out_specs=[VMEM, VMEM],
        out_shape=[pltpu.VMEM(shape, F32), pltpu.VMEM(shape, BF16)],
        scratch_shapes=[
            pltpu.VMEM((Y, 2, 2, 128, 256), BF16),
            pltpu.VMEM((Y, 2, 1024, 128), BF16),
            pltpu.VMEM((Y, 9, 2, 128), BF16),
            pltpu.SemaphoreType.DMA((3, Y)),
        ],
        compiler_params=pltpu.CompilerParams(vmem_limit_bytes=16 << 20),
        name="pack",
    )(in_hbm(expert_grads), in_hbm(embed_grads), in_hbm(small_grads[:, 0].transpose(2, 0, 1)))


def kernel_in_vmem(kernel, name, shapes, *args):
    return pl.pallas_call(
        kernel,
        in_specs=[VMEM] * len(args),
        out_specs=[VMEM] * len(shapes),
        out_shape=[pltpu.VMEM(*shape) for shape in shapes],
        compiler_params=pltpu.CompilerParams(vmem_limit_bytes=16 << 20),
        name=name,
    )(*(in_vmem(x) for x in args))


def pair_kernel(keep_ref, got_ref, out_ref):
    @pl.loop(0, A)
    def _(a):
        out_ref[a, :MAIN] = (keep_ref[a, :MAIN] + got_ref[a, :MAIN].astype(F32)).astype(BF16)
        small = got_ref[a, MAIN:].astype(F32)
        small = keep_ref[a, MAIN:] + (small + flip(small))
        out_ref[a, MAIN:] = two_terms(small).astype(BF16)


def add_pair(keep, got):
    return kernel_in_vmem(pair_kernel, "add_pair", [((A, MSG, 128), BF16)], keep, got)[0]


def near_kernel(got_ref, out_ref):
    def total(rows):
        out = got_ref[0, rows].astype(F32)
        for a in range(1, A):
            out = out + got_ref[a, rows].astype(F32)
        return out

    shared = total(slice(MAIN, MSG))
    shared = shared + flip(shared)
    for z in range(ZH):
        out_ref[PLACE[z], :SMA] = total(slice(z * SMA, z * SMA + SMA)).astype(BF16)
        out_ref[PLACE[z], SMA:] = two_terms(nine(shift(shared, z, True))).astype(BF16)


def add_near(got):
    return kernel_in_vmem(near_kernel, "add_near", [((ZH, ROWS, 128), BF16)], got)[0]


def spread_kernel(own_ref, out_ref):
    shared = jnp.zeros((8, 128), F32)
    for z in range(ZH):
        main = own_ref[PLACE[z], :SMA]
        for a in range(A):
            out_ref[a, z * SMA : z * SMA + SMA] = main
        shared = shared + shift(nine(own_ref[PLACE[z], SMA:].astype(F32)), z)
    for a in range(A):
        out_ref[a, MAIN:] = shared.astype(BF16)


def spread(own):
    return kernel_in_vmem(spread_kernel, "spread", [((A, MSG, 128), BF16)], own)[0]


def far_kernel(got_ref, total_ref, line_ref):
    total = got_ref[0].astype(F32)
    for k in range(1, ZH):
        total = total + got_ref[k].astype(F32)
    small = total[SMA:] + flip(total[SMA:])
    total_ref[:SMA] = total[:SMA]
    total_ref[SMA:] = small
    squares = jnp.sum(total[:SMA] * total[:SMA]) + 0.5 * jnp.sum(small * small)
    line_ref[...] = jnp.full(line_ref.shape, squares, F32)


def add_far(got):
    return kernel_in_vmem(
        far_kernel, "add_far", [((ROWS, 128), F32), ((A * C * T, 128), F32)], got
    )


def update(scaled, first, second, master, corr_one, corr_two):
    first_new = BETA_ONE * first + (1.0 - BETA_ONE) * scaled
    second_new = BETA_TWO * second + (1.0 - BETA_TWO) * scaled * scaled
    step = (
        first_new / corr_one / (jnp.sqrt(second_new / corr_two) + EPSILON) + DECAY_RATE * master
    )
    return first_new, second_new, step, master - LEARN_RATE * step


def adam_kernel(
    line_ref,
    total_ref,
    rms_ref,
    corr_ref,
    exp_m,
    exp_f,
    exp_s,
    emb_m,
    emb_f,
    emb_s,
    sma_m,
    sma_f,
    sma_s,
    weights_ref,
    exp_mo,
    exp_fo,
    exp_so,
    emb_mo,
    emb_fo,
    emb_so,
    emb_step,
    sma_mo,
    sma_fo,
    sma_so,
    clip_ref,
):
    fixed = (1.0 - BETA_ONE**STEP, 1.0 - BETA_TWO**STEP)
    squares = jnp.sum(line_ref[...], axis=0, keepdims=True)
    factor = rms_ref[...] * jnp.sqrt(P_TOT / squares)
    clip_ref[...] = factor
    first, second, step, master = update(
        factor * total_ref[:EMB], emb_f[...], emb_s[...], emb_m[...], corr_ref[0], corr_ref[1]
    )
    emb_fo[...], emb_so[...], emb_step[...], emb_mo[...] = first, second, step, master
    chunks = [master.astype(BF16).astype(F32)]
    for m in range(2):
        halves = []
        for h in range(2):
            at = (m, slice(None), slice(128 * h, 128 * h + 128))
            row = EMB + 8 * m + 4 * h
            first, second, _, master = update(
                factor * total_ref[row : row + 4], exp_f[at], exp_s[at], exp_m[at], *fixed
            )
            exp_fo[at], exp_so[at], exp_mo[at] = first, second, master
            halves.append(master)
        chunks.append(jnp.concatenate(halves, axis=0))
    first, second, _, master = update(
        factor[:, :9] * total_ref[SMA : SMA + 4, :9], sma_f[...], sma_s[...], sma_m[...], *fixed
    )
    sma_fo[...], sma_so[...], sma_mo[...] = first, second, master
    wide = jnp.concatenate([master, jnp.zeros((4, 128 - 9), F32)], axis=1)
    chunks.append(jnp.concatenate([wide, jnp.zeros((4, 128), F32)], axis=0))
    chunk = jnp.concatenate(chunks, axis=0).astype(BF16)
    for a in range(ZH):
        weights_ref[a] = chunk


def adam(line, total, rms, corr, states):
    shapes = [(ZH, ROWS, 128)] + [(2, 4, 256)] * 3 + [(32, 128)] * 4 + [(4, 9)] * 3 + [(1, 128)]
    out = [jax.ShapeDtypeStruct(n, F32) for n in shapes]
    out[0] = pltpu.VMEM(shapes[0], BF16)
    return pl.pallas_call(
        adam_kernel,
        in_specs=[VMEM] * 13,
        out_specs=[VMEM] * len(out),
        out_shape=out,
        compiler_params=pltpu.CompilerParams(vmem_limit_bytes=16 << 20),
        name="adam",
    )(line, total, rms, corr, *states)


def unpack_kernel(own_ref, other_ref, expert_ref, embed_ref, small_ref):
    for core in range(C):

        @pl.when(lax.axis_index("c") == core)
        def _():
            pair = (own_ref, other_ref) if core == 0 else (other_ref, own_ref)
            unpack_rows(pair, expert_ref, embed_ref, small_ref)


def unpack_rows(refs, expert_ref, embed_ref, small_ref):
    y = pl.program_id(0)
    upper = low_rows((8, 128))
    tiles = [None] * (ZH * W)
    for w in range(W):
        shared = [ref[y * W + w, MAIN:].astype(F32) for ref in refs]
        shared = jnp.where(upper, shared[0], flip(shared[1]))
        for z in range(ZH):
            pair = [ref[y * W + w, z * SMA : z * SMA + SMA] for ref in refs]
            base = (z * W + w) * C * EMB
            for c in range(C):
                embed_ref[pl.ds(base + c * EMB, EMB), :] = pair[c][:EMB]
            row = (z * W + w) * 8
            for m in range(2):
                zero, one = (p[EMB + 8 * m : EMB + 8 * m + 8].astype(F32) for p in pair)
                expert_ref[m, pl.ds(row, 8), :128] = jnp.where(upper, zero, flip(one)).astype(BF16)
                expert_ref[m, pl.ds(row, 8), 128:] = jnp.where(upper, flip(zero), one).astype(BF16)
            tiles[z * W + w] = shift(shared, z, True)
    small_ref[...] = jnp.concatenate(tiles, axis=0).T[:9].astype(BF16)


def unpack(own, other):
    expert, embed, small = pl.pallas_call(
        unpack_kernel,
        grid=(Y,),
        in_specs=[VMEM, VMEM],
        out_specs=[
            pl.BlockSpec((2, 128, 256), lambda y: (0, y, 0)),
            pl.BlockSpec((1024, 128), lambda y: (y, 0)),
            pl.BlockSpec((9, 128), lambda y: (0, y)),
        ],
        out_shape=[
            jax.ShapeDtypeStruct((2, 512, 256), BF16),
            jax.ShapeDtypeStruct((4096, 128), BF16),
            jax.ShapeDtypeStruct((9, 512), BF16),
        ],
        compiler_params=pltpu.CompilerParams(vmem_limit_bytes=16 << 20),
        name="unpack",
    )(in_vmem(own), in_vmem(other))
    return expert, embed, small.T


def exchange(x, axes):
    return lax.all_to_all(x, axes, 0, 0, tiled=True)


ORDER = (4, 5, 6, 7, 0, 1, 2, 3)
PLACE = tuple(ORDER.index(z) for z in range(ZH))


def exchange_far(x):
    return lax.all_to_all(x, "z", 0, 0, tiled=True, axis_index_groups=[ORDER])


def body(
    expert_grads,
    embed_grads,
    small_grads,
    expert_master,
    expert_first,
    expert_second,
    embed_master,
    embed_first,
    embed_second,
    small_master,
    small_first,
    small_second,
    class_steps,
    clip_rms,
):
    row_float = class_steps.astype(F32)[:, None]
    corr = jnp.stack([1.0 - BETA_ONE**row_float, 1.0 - BETA_TWO**row_float])
    corr = jnp.broadcast_to(corr, (2, EMB, 128))
    keep, send = pack(expert_grads, embed_grads, small_grads)
    rms = jnp.broadcast_to(clip_rms, (1, 128))
    got, corr, rms = lax.optimization_barrier((lax.ppermute(send, "c", SWAP), corr, rms))
    far = add_near(exchange(add_pair(keep, got), NEAR))
    total, line = add_far(exchange_far(far))
    line = jnp.sum(exchange(line, NEAR + ("c", "t")), axis=0)
    line = exchange_far(jnp.broadcast_to(line, (ZH, 128)))
    states = (
        expert_master,
        expert_first,
        expert_second,
        embed_master,
        embed_first,
        embed_second,
        small_master,
        small_first,
        small_second,
    )
    weights, *new, clip = adam(line, total, rms, corr, states)
    own = exchange_far(weights)
    own = exchange(spread(own), NEAR)
    expert_w, embed_w, small_w = unpack(own, lax.ppermute(own, "c", SWAP))
    return (expert_w, embed_w, small_w, *new, clip[0, 0])


def solution(mesh):
    fine = Mesh(mesh.devices.reshape(Y, ZH, W, C, T), ("y", "z", "w", "c", "t"))
    sh = ("y", "z", "w", "c")
    in_specs = (
        P(None, sh, None, None, "t"),
        P(None, sh, None, "t"),
        P(None, sh, None, "t"),
        P(None, sh, "t"),
        P(None, sh, "t"),
        P(None, sh, "t"),
        P(sh, "t"),
        P(sh, "t"),
        P(sh, "t"),
        P(sh, "t"),
        P(sh, "t"),
        P(sh, "t"),
        P(sh),
        P(),
    )
    out_specs = (
        P(None, None, "t"),
        P(None, "t"),
        P(None, "t"),
        P(None, sh, "t"),
        P(None, sh, "t"),
        P(None, sh, "t"),
        P(sh, "t"),
        P(sh, "t"),
        P(sh, "t"),
        P(sh, "t"),
        P(sh, "t"),
        P(sh, "t"),
        P(sh, "t"),
        P(),
    )
    return jax.shard_map(body, mesh=fine, in_specs=in_specs, out_specs=out_specs, check_vma=False)
```

```python
import jax
import jax.numpy as jnp
from jax import lax
from jax.experimental import pallas as pl
from jax.experimental.pallas import tpu as pltpu
from jax.sharding import Mesh, PartitionSpec as P

STEP = 1000
P_TOT = 3164160

BETA_ONE = 0.9
BETA_TWO = 0.999
LEARN_RATE = 0.001
DECAY_RATE = 0.1
EPSILON = 1e-08

Y, ZH, W, C, T = 4, 8, 2, 2, 4
A = Y * W
NEAR = ("y", "w")
EMB, EXP, ROWS = 32, 16, 56
SMA = EMB + EXP
MAIN, MSG = ZH * SMA, ZH * SMA + 8
SWAP = ((0, 1), (1, 0))
F32, BF16 = jnp.float32, jnp.bfloat16
VMEM = pl.BlockSpec(memory_space=pltpu.VMEM)


def in_hbm(x):
    return pltpu.with_memory_space_constraint(x, pltpu.HBM)


def in_vmem(x):
    return pltpu.with_memory_space_constraint(x, pltpu.VMEM)


def low_rows(shape):
    return lax.broadcasted_iota(jnp.int32, shape, len(shape) - 2) < 4


def flip(x):
    return pltpu.roll(x, 4, x.ndim - 2)


def shift(x, z, back=False):
    return pltpu.roll(x, (128 - 9 * z) % 128 if back else 9 * z, x.ndim - 1)


def nine(x):
    return jnp.where(lax.broadcasted_iota(jnp.int32, x.shape, x.ndim - 1) < 9, x, 0.0)


def two_terms(x):
    high = x.astype(BF16).astype(F32)
    return jnp.where(low_rows(x.shape), high, flip(x - high))


def pack_kernel(expert_hbm, embed_hbm, small_hbm, keep_ref, send_ref, expert, embed, small, sems):
    def copies(y):
        rows = embed_hbm.at[:, 0, pl.ds(y * 1024, 1024)]
        tiles = expert_hbm.at[:, 0, :, pl.ds(y * 128, 128)]
        lanes = small_hbm.at[:, :, pl.ds(y * 128, 128)]
        return [
            pltpu.make_async_copy(rows, embed.at[y], sems.at[0, y]),
            pltpu.make_async_copy(tiles, expert.at[y], sems.at[1, y]),
            pltpu.make_async_copy(lanes, small.at[y], sems.at[2, y]),
        ]

    for y in range(Y):
        for copy in copies(y):
            copy.start()

    @pl.loop(0, Y)
    def _(y):
        for copy in copies(y):
            copy.wait()
        for core in range(C):

            @pl.when(lax.axis_index("c") == core)
            def _():
                pack_rows(core, y, expert, embed, small, keep_ref, send_ref)


def pack_rows(core, y, expert_ref, embed_ref, small_ref, keep_ref, send_ref):
    def put(w, row, rows, *values):
        at = (y * W + w, pl.ds(row, rows))
        keep_ref[at] = values[core]
        send_ref[at] = values[1 - core].astype(BF16)

    small = small_ref[y, :, 0, :].astype(F32) + small_ref[y, :, 1, :].astype(F32)
    small = jnp.concatenate([small, jnp.zeros((128 - 9, 128), F32)], axis=0).T
    for w in range(W):
        shared = jnp.zeros((8, 128), F32)
        for z in range(ZH):
            base = (z * W + w) * C * EMB
            pair = [
                embed_ref[y, 0, pl.ds(base + c * EMB, EMB), :].astype(F32)
                + embed_ref[y, 1, pl.ds(base + c * EMB, EMB), :].astype(F32)
                for c in range(C)
            ]
            put(w, z * SMA, EMB, *pair)
            row = (z * W + w) * 8
            for m in range(2):
                tile = expert_ref[y, 0, m, pl.ds(row, 8), :].astype(F32) + expert_ref[
                    y, 1, m, pl.ds(row, 8), :
                ].astype(F32)
                left, right = tile[:, :128], tile[:, 128:]
                upper = low_rows((8, 128))
                put(
                    w,
                    z * SMA + EMB + 8 * m,
                    8,
                    jnp.where(upper, left, flip(right)),
                    jnp.where(upper, flip(left), right),
                )
            shared = shared + shift(small[row : row + 8], z)
        pair = [shared, flip(shared)]
        pair[1 - core] = two_terms(pair[1 - core])
        put(w, MAIN, 8, *pair)


def pack(expert_grads, embed_grads, small_grads):
    shape = (A, MSG, 128)
    return pl.pallas_call(
        pack_kernel,
        in_specs=[pl.BlockSpec(memory_space=pltpu.HBM)] * 3,
        out_specs=[VMEM, VMEM],
        out_shape=[pltpu.VMEM(shape, F32), pltpu.VMEM(shape, BF16)],
        scratch_shapes=[
            pltpu.VMEM((Y, 2, 2, 128, 256), BF16),
            pltpu.VMEM((Y, 2, 1024, 128), BF16),
            pltpu.VMEM((Y, 9, 2, 128), BF16),
            pltpu.SemaphoreType.DMA((3, Y)),
        ],
        compiler_params=pltpu.CompilerParams(vmem_limit_bytes=16 << 20),
        name="pack",
    )(in_hbm(expert_grads), in_hbm(embed_grads), in_hbm(small_grads[:, 0].transpose(2, 0, 1)))


def kernel_in_vmem(kernel, name, shapes, *args):
    return pl.pallas_call(
        kernel,
        in_specs=[VMEM] * len(args),
        out_specs=[VMEM] * len(shapes),
        out_shape=[pltpu.VMEM(*shape) for shape in shapes],
        compiler_params=pltpu.CompilerParams(vmem_limit_bytes=16 << 20),
        name=name,
    )(*(in_vmem(x) for x in args))


def pair_kernel(keep_ref, got_ref, out_ref):
    @pl.loop(0, A)
    def _(a):
        place = lax.rem(a + A // 2, A)
        out_ref[place, :MAIN] = (keep_ref[a, :MAIN] + got_ref[a, :MAIN].astype(F32)).astype(BF16)
        small = got_ref[a, MAIN:].astype(F32)
        small = keep_ref[a, MAIN:] + (small + flip(small))
        out_ref[place, MAIN:] = two_terms(small).astype(BF16)


def add_pair(keep, got):
    return kernel_in_vmem(pair_kernel, "add_pair", [((A, MSG, 128), BF16)], keep, got)[0]


def near_kernel(got_ref, out_ref):
    def total(rows):
        out = got_ref[0, rows].astype(F32)
        for a in range(1, A):
            out = out + got_ref[a, rows].astype(F32)
        return out

    shared = total(slice(MAIN, MSG))
    shared = shared + flip(shared)
    for z in range(ZH):
        out_ref[PLACE[z], :SMA] = total(slice(z * SMA, z * SMA + SMA)).astype(BF16)
        out_ref[PLACE[z], SMA:] = two_terms(nine(shift(shared, z, True))).astype(BF16)


def add_near(got):
    return kernel_in_vmem(near_kernel, "add_near", [((ZH, ROWS, 128), BF16)], got)[0]


def spread_kernel(own_ref, out_ref):
    shared = jnp.zeros((8, 128), F32)
    for z in range(ZH):
        main = own_ref[PLACE[z], :SMA]
        for a in range(A):
            out_ref[a, z * SMA : z * SMA + SMA] = main
        shared = shared + shift(nine(own_ref[PLACE[z], SMA:].astype(F32)), z)
    for a in range(A):
        out_ref[a, MAIN:] = shared.astype(BF16)


def spread(own):
    return kernel_in_vmem(spread_kernel, "spread", [((A, MSG, 128), BF16)], own)[0]


def far_kernel(got_ref, total_ref, line_ref):
    total = got_ref[0].astype(F32)
    for k in range(1, ZH):
        total = total + got_ref[k].astype(F32)
    small = total[SMA:] + flip(total[SMA:])
    total_ref[:SMA] = total[:SMA]
    total_ref[SMA:] = small
    squares = jnp.sum(total[:SMA] * total[:SMA]) + 0.5 * jnp.sum(small * small)
    line_ref[...] = jnp.full(line_ref.shape, squares, F32)


def add_far(got):
    return kernel_in_vmem(
        far_kernel, "add_far", [((ROWS, 128), F32), ((A * C * T, 128), F32)], got
    )


def update(scaled, first, second, master, corr_one, corr_two):
    first_new = BETA_ONE * first + (1.0 - BETA_ONE) * scaled
    second_new = BETA_TWO * second + (1.0 - BETA_TWO) * scaled * scaled
    step = (
        first_new / corr_one / (jnp.sqrt(second_new / corr_two) + EPSILON) + DECAY_RATE * master
    )
    return first_new, second_new, step, master - LEARN_RATE * step


def adam_kernel(
    line_ref,
    total_ref,
    rms_ref,
    corr_ref,
    exp_m,
    exp_f,
    exp_s,
    emb_m,
    emb_f,
    emb_s,
    sma_m,
    sma_f,
    sma_s,
    weights_ref,
    exp_mo,
    exp_fo,
    exp_so,
    emb_mo,
    emb_fo,
    emb_so,
    emb_step,
    sma_mo,
    sma_fo,
    sma_so,
    clip_ref,
):
    fixed = (1.0 - BETA_ONE**STEP, 1.0 - BETA_TWO**STEP)
    squares = jnp.sum(line_ref[...], axis=0, keepdims=True)
    factor = rms_ref[...] * jnp.sqrt(P_TOT / squares)
    clip_ref[...] = factor
    first, second, step, master = update(
        factor * total_ref[:EMB], emb_f[...], emb_s[...], emb_m[...], corr_ref[0], corr_ref[1]
    )
    emb_fo[...], emb_so[...], emb_step[...], emb_mo[...] = first, second, step, master
    chunks = [master.astype(BF16).astype(F32)]
    for m in range(2):
        halves = []
        for h in range(2):
            at = (m, slice(None), slice(128 * h, 128 * h + 128))
            row = EMB + 8 * m + 4 * h
            first, second, _, master = update(
                factor * total_ref[row : row + 4], exp_f[at], exp_s[at], exp_m[at], *fixed
            )
            exp_fo[at], exp_so[at], exp_mo[at] = first, second, master
            halves.append(master)
        chunks.append(jnp.concatenate(halves, axis=0))
    first, second, _, master = update(
        factor[:, :9] * total_ref[SMA : SMA + 4, :9], sma_f[...], sma_s[...], sma_m[...], *fixed
    )
    sma_fo[...], sma_so[...], sma_mo[...] = first, second, master
    wide = jnp.concatenate([master, jnp.zeros((4, 128 - 9), F32)], axis=1)
    chunks.append(jnp.concatenate([wide, jnp.zeros((4, 128), F32)], axis=0))
    chunk = jnp.concatenate(chunks, axis=0).astype(BF16)
    for a in range(ZH):
        weights_ref[a] = chunk


def adam(line, total, rms, corr, states):
    shapes = [(ZH, ROWS, 128)] + [(2, 4, 256)] * 3 + [(32, 128)] * 4 + [(4, 9)] * 3 + [(1, 128)]
    out = [jax.ShapeDtypeStruct(n, F32) for n in shapes]
    out[0] = pltpu.VMEM(shapes[0], BF16)
    return pl.pallas_call(
        adam_kernel,
        in_specs=[VMEM] * 13,
        out_specs=[VMEM] * len(out),
        out_shape=out,
        compiler_params=pltpu.CompilerParams(vmem_limit_bytes=16 << 20),
        name="adam",
    )(line, total, rms, corr, *states)


def unpack_kernel(own_ref, other_ref, expert_ref, embed_ref, small_ref):
    for core in range(C):

        @pl.when(lax.axis_index("c") == core)
        def _():
            pair = (own_ref, other_ref) if core == 0 else (other_ref, own_ref)
            unpack_rows(pair, expert_ref, embed_ref, small_ref)


def unpack_rows(refs, expert_ref, embed_ref, small_ref):
    y = lax.rem(pl.program_id(0) + Y // 2, Y)
    upper = low_rows((8, 128))
    tiles = [None] * (ZH * W)
    for w in range(W):
        shared = [ref[y * W + w, MAIN:].astype(F32) for ref in refs]
        shared = jnp.where(upper, shared[0], flip(shared[1]))
        for z in range(ZH):
            pair = [ref[y * W + w, z * SMA : z * SMA + SMA] for ref in refs]
            base = (z * W + w) * C * EMB
            for c in range(C):
                embed_ref[pl.ds(base + c * EMB, EMB), :] = pair[c][:EMB]
            row = (z * W + w) * 8
            for m in range(2):
                zero, one = (p[EMB + 8 * m : EMB + 8 * m + 8].astype(F32) for p in pair)
                expert_ref[m, pl.ds(row, 8), :128] = jnp.where(upper, zero, flip(one)).astype(BF16)
                expert_ref[m, pl.ds(row, 8), 128:] = jnp.where(upper, flip(zero), one).astype(BF16)
            tiles[z * W + w] = shift(shared, z, True)
    small_ref[...] = jnp.concatenate(tiles, axis=0).T[:9].astype(BF16)


def unpack(own, other):
    expert, embed, small = pl.pallas_call(
        unpack_kernel,
        grid=(Y,),
        in_specs=[VMEM, VMEM],
        out_specs=[
            pl.BlockSpec((2, 128, 256), lambda y: (0, y, 0)),
            pl.BlockSpec((1024, 128), lambda y: (y, 0)),
            pl.BlockSpec((9, 128), lambda y: (0, y)),
        ],
        out_shape=[
            jax.ShapeDtypeStruct((2, 512, 256), BF16),
            jax.ShapeDtypeStruct((4096, 128), BF16),
            jax.ShapeDtypeStruct((9, 512), BF16),
        ],
        compiler_params=pltpu.CompilerParams(vmem_limit_bytes=16 << 20),
        name="unpack",
    )(in_vmem(own), in_vmem(other))
    return expert, embed, small.T


def exchange(x, axes):
    half = x.shape[0] // 2
    order = [*range(half, 2 * half), *range(half)]
    return lax.all_to_all(x, axes, 0, 0, tiled=True, axis_index_groups=[order])


ORDER = (4, 5, 6, 7, 0, 1, 2, 3)
PLACE = tuple(ORDER.index(z) for z in range(ZH))


def exchange_far(x):
    return lax.all_to_all(x, "z", 0, 0, tiled=True, axis_index_groups=[ORDER])


def body(
    expert_grads,
    embed_grads,
    small_grads,
    expert_master,
    expert_first,
    expert_second,
    embed_master,
    embed_first,
    embed_second,
    small_master,
    small_first,
    small_second,
    class_steps,
    clip_rms,
):
    row_float = class_steps.astype(F32)[:, None]
    corr = jnp.stack([1.0 - BETA_ONE**row_float, 1.0 - BETA_TWO**row_float])
    corr = jnp.broadcast_to(corr, (2, EMB, 128))
    keep, send = pack(expert_grads, embed_grads, small_grads)
    rms = jnp.broadcast_to(clip_rms, (1, 128))
    got, corr, rms = lax.optimization_barrier((lax.ppermute(send, "c", SWAP), corr, rms))
    far = add_near(exchange(add_pair(keep, got), NEAR))
    total, line = add_far(exchange_far(far))
    line = jnp.sum(exchange(line, NEAR + ("c", "t")), axis=0)
    line = exchange_far(jnp.broadcast_to(line, (ZH, 128)))
    states = (
        expert_master,
        expert_first,
        expert_second,
        embed_master,
        embed_first,
        embed_second,
        small_master,
        small_first,
        small_second,
    )
    weights, *new, clip = adam(line, total, rms, corr, states)
    own = exchange_far(weights)
    own = exchange(spread(own), NEAR)
    expert_w, embed_w, small_w = unpack(own, lax.ppermute(own, "c", SWAP))
    return (expert_w, embed_w, small_w, *new, clip[0, 0])


def solution(mesh):
    fine = Mesh(mesh.devices.reshape(Y, ZH, W, C, T), ("y", "z", "w", "c", "t"))
    sh = ("y", "z", "w", "c")
    in_specs = (
        P(None, sh, None, None, "t"),
        P(None, sh, None, "t"),
        P(None, sh, None, "t"),
        P(None, sh, "t"),
        P(None, sh, "t"),
        P(None, sh, "t"),
        P(sh, "t"),
        P(sh, "t"),
        P(sh, "t"),
        P(sh, "t"),
        P(sh, "t"),
        P(sh, "t"),
        P(sh),
        P(),
    )
    out_specs = (
        P(None, None, "t"),
        P(None, "t"),
        P(None, "t"),
        P(None, sh, "t"),
        P(None, sh, "t"),
        P(None, sh, "t"),
        P(sh, "t"),
        P(sh, "t"),
        P(sh, "t"),
        P(sh, "t"),
        P(sh, "t"),
        P(sh, "t"),
        P(sh, "t"),
        P(),
    )
    return jax.shard_map(body, mesh=fine, in_specs=in_specs, out_specs=out_specs, check_vma=False)
```
